32 devices in a mesh: groups: 2 (over y), tile: 16 (over z, x, core).
Axes of the slice: x: 2, y: 2, z: 4, core: 2. Of those that a mesh axis runs over, the one named last changes fastest.
Arguments:
- coarse: bfloat16 [12, 512, 512], P(None, ('groups', 'tile')), parts along dimension 1, may hold values from -6 to 6
- noise_field: bfloat16 [2, 12, 512, 512], P(None, None, ('groups', 'tile')), parts along dimension 2, may hold values from -6 to 6
- anchors: int32 [32, 2], P(('groups', 'tile')), parts along dimension 0, may hold values from 0 to 288
- counts: int32 [32], P(('groups', 'tile')), parts along dimension 0, may hold values from 1 to 2, as said below
- blend_weights: int32 [224, 224], replicated, may hold values from 1 to 16
- regress_lift: bfloat16 [12, 128], replicated, may hold values from -1.75 to 1.75
- regress_conv: bfloat16 [2, 9, 128, 128], replicated, may hold values from -0.1875 to 0.1875
- regress_head: bfloat16 [128, 12], replicated, may hold values from -0.5 to 0.5
- denoise_lift: bfloat16 [36, 128], replicated, may hold values from -1 to 1
- denoise_conv: bfloat16 [2, 9, 128, 128], replicated, may hold values from -0.1875 to 0.1875
- denoise_head: bfloat16 [128, 12], replicated, may hold values from -0.5 to 0.5
Outputs:
- ens_mean: float32 [12, 512, 512], P(None, ('groups', 'tile')), parts along dimension 1
- ens_var: float32 [12, 512, 512], P(None, ('groups', 'tile')), parts along dimension 1
The draws below stay inside these ranges and needn't reach their ends.
There are 2 independent parts, one for each index of `groups`. The reference program is written for one: setup_inputs(seed, part) draws one part's arguments, and reference() takes and returns one part's arrays. A program takes and returns all parts, laid end to end along the dimension named above; an argument that names none is the same for every part. Nothing has to cross between parts.
Inputs may be any that keep to these rules, and one draw needn't show every extreme that they name: The first counts[s] slots of strip s are live; some strip has all 2 live in every draw.
All inputs are finite; a program needn't handle non-finite values.
Results may differ from the reference program's by a relative error of at most 0.0034.
Values may be sent and summed in bfloat16 or wider, within the bound.
A program may use at most 320 MiB of HBM per device.

```python
import math
import jax
import jax.numpy as jnp
from jax import lax

CH = 12
WIDTH = 128
STRIP = 16
COLS = 512
PATCH = 224
POOL = 4
SLOTS = 2
MEMBERS = 2
REG_LAYERS = 2
DEN_LAYERS = 2
WEIGHT_LEVELS = 16
ROWS = 256
N_TILE = 16


def draw_counts(key, part):
    key_low, key_heavy, key_pick = jax.random.split(key, 3)
    low_counts = jax.random.randint(key_low, (N_TILE,), 1, 3)
    heavy_flag = jax.random.randint(key_heavy, (N_TILE,), 0, 4) == 0
    drawn = jnp.where(heavy_flag, SLOTS, jnp.minimum(low_counts, SLOTS))
    picked = jax.random.randint(key_pick, (), 0, N_TILE)
    drawn = drawn.at[picked].set(SLOTS)
    return drawn.astype(jnp.int32)


def plant(array, rng, low, high):
    longest = array.shape.index(max(array.shape))
    spots = []
    for shift in (0, 1):
        where = [jax.random.randint(jax.random.fold_in(rng, axis), (), 0, length) for axis, length in enumerate(array.shape)]
        where[longest] = (where[longest] + shift) % array.shape[longest]
        spots.append(tuple(where))
    return array.at[spots[0]].set(low).at[spots[1]].set(high)


def level_of(key, extent, cuts, least, largest):
    gain = 1.0
    for axis_at, shards_of in cuts:
        steps = jax.random.uniform(jax.random.fold_in(jax.random.fold_in(key, 6), axis_at), (shards_of,), jnp.float32, least / len(cuts), largest / len(cuts))
        gain = gain * jnp.repeat(jnp.exp(steps), extent[axis_at] // shards_of).reshape((-1,) + (1,) * (len(extent) - 1 - axis_at))
    return gain


def scatter_about(rng, dims, spread, bound, cuts=(), kind=jnp.bfloat16):
    loudness = level_of(rng, dims, cuts, -0.22, 0.18) if cuts else 1.0
    values = jax.random.normal(rng, dims, jnp.float32) * spread * loudness
    return jnp.minimum(jnp.maximum(values, -bound), bound).astype(kind)


def setup_inputs(seed: int = 0, part: int = 0) -> dict:
    streams_of = jax.random.split(jax.random.key(seed), 12)
    part_splits = jax.random.split(jax.random.fold_in(streams_of[11], part), 12)
    return {
        "coarse": scatter_about(part_splits[0], (CH, ROWS, COLS), 1.0, 6.0, ((1, 16),)),
        "noise_field": scatter_about(part_splits[1], (MEMBERS, CH, ROWS, COLS), 1.0, 6.0, ((2, 16),)),
        "anchors": plant(jax.random.randint(part_splits[2], (N_TILE, SLOTS), 0, COLS - PATCH + 1), jax.random.fold_in(part_splits[2], 1), 0, COLS - PATCH).astype(jnp.int32),
        "counts": draw_counts(jax.random.fold_in(jax.random.fold_in(streams_of[11], part), 71), part),
        "blend_weights": plant(jax.random.randint(streams_of[4], (PATCH, PATCH), 1, WEIGHT_LEVELS + 1), jax.random.fold_in(streams_of[4], 1), 1, WEIGHT_LEVELS).astype(jnp.int32),
        "regress_lift": scatter_about(streams_of[5], (CH, WIDTH), CH ** -0.5, 1.75),
        "regress_conv": scatter_about(streams_of[6], (REG_LAYERS, 9, WIDTH, WIDTH), (9 * WIDTH) ** -0.5, 0.1875),
        "regress_head": scatter_about(streams_of[7], (WIDTH, CH), WIDTH ** -0.5, 0.5),
        "denoise_lift": scatter_about(streams_of[8], (3 * CH, WIDTH), (3 * CH) ** -0.5, 1.0),
        "denoise_conv": scatter_about(streams_of[9], (DEN_LAYERS, 9, WIDTH, WIDTH), (9 * WIDTH) ** -0.5, 0.1875),
        "denoise_head": scatter_about(streams_of[10], (WIDTH, CH), WIDTH ** -0.5, 0.5),
    }


skip_gain = 0.2
out_gain = 0.5 / math.sqrt(1.25)
in_gain = 1.0 / math.sqrt(1.25)

def block_mean(field):
    lead = field.shape[:-2]
    row_count = field.shape[-2] // POOL
    col_count = field.shape[-1] // POOL
    grouped = field.astype(jnp.float32).reshape(lead + (row_count, POOL, col_count, POOL))
    return lax.optimization_barrier(jnp.mean(grouped, axis=(-3, -1)))

def spread_blocks(field):
    lead = field.shape[:-2]
    row_count = field.shape[-2]
    col_count = field.shape[-1]
    wide = jnp.broadcast_to(field[..., :, None, :, None], lead + (row_count, POOL, col_count, POOL))
    return wide.reshape(lead + (row_count * POOL, col_count * POOL))

def conv_cells(padded, kernel):
    row_count = padded.shape[1] - 2
    col_count = padded.shape[2] - 2
    feat_count = padded.shape[3]
    flat_kernel = kernel.reshape(9 * feat_count, kernel.shape[2])

    def conv_item(item):
        taps = [item[shift_row:shift_row + row_count, shift_col:shift_col + col_count, :] for shift_row in range(3) for shift_col in range(3)]
        stacked = jnp.concatenate(taps, axis=-1).reshape(-1, 9 * feat_count)
        return jnp.dot(stacked, flat_kernel, preferred_element_type=jnp.float32).reshape(row_count, col_count, kernel.shape[2])
    return lax.map(conv_item, padded)

def conv_same(hidden_act, kernel):
    padded = jnp.pad(hidden_act, ((0, 0), (1, 1), (1, 1), (0, 0)))
    return conv_cells(padded, kernel)

def residual_layer(hidden_act, conv_term):
    return (hidden_act.astype(jnp.float32) + jax.nn.silu(conv_term)).astype(jnp.bfloat16)

def denoise(noise_patch, cond_patch, denoise_lift, denoise_conv, denoise_head):
    channel_count = noise_patch.shape[2]
    noise_low = block_mean(noise_patch).astype(jnp.bfloat16)
    cond_low = block_mean(cond_patch).astype(jnp.bfloat16)
    lifted = in_gain * jnp.einsum('bmcij,ck->bmijk', noise_low.astype(jnp.float32), denoise_lift[:channel_count].astype(jnp.float32))
    lifted = lifted + jnp.einsum('bcij,ck->bijk', cond_low.astype(jnp.float32), denoise_lift[channel_count:].astype(jnp.float32))[:, None]
    hidden_act = lifted.astype(jnp.bfloat16)
    act_shape = hidden_act.shape
    flat_act = hidden_act.reshape((-1,) + act_shape[2:])
    for layer_index in range(denoise_conv.shape[0]):
        flat_act = residual_layer(flat_act, conv_same(flat_act, denoise_conv[layer_index]))
    head_term = jnp.einsum('nijk,kc->ncij', flat_act.astype(jnp.float32), denoise_head.astype(jnp.float32))
    head_term = head_term.reshape(act_shape[0], act_shape[1], channel_count, act_shape[2], act_shape[3])
    return skip_gain * noise_patch.astype(jnp.float32) + out_gain * spread_blocks(head_term)

def reference(coarse, noise_field, anchors, counts, blend_weights, regress_lift, regress_conv, regress_head, denoise_lift, denoise_conv, denoise_head):
    coarse_low = block_mean(coarse).astype(jnp.bfloat16)
    hidden_act = jnp.einsum('crw,ck->rwk', coarse_low.astype(jnp.float32), regress_lift.astype(jnp.float32))[None].astype(jnp.bfloat16)
    for layer_index in range(regress_conv.shape[0]):
        hidden_act = residual_layer(hidden_act, conv_same(hidden_act, regress_conv[layer_index]))
    reg_low = jnp.einsum('rwk,kc->crw', hidden_act[0].astype(jnp.float32), regress_head.astype(jnp.float32))
    reg_mean = coarse.astype(jnp.float32) + spread_blocks(reg_low)
    condition = jnp.concatenate([reg_mean.astype(jnp.bfloat16), coarse], axis=0)
    noise_pad = jnp.pad(noise_field, ((0, 0), (0, 0), (0, PATCH), (0, 0)))
    cond_pad = jnp.pad(condition, ((0, 0), (0, PATCH), (0, 0)))
    weight_tile = blend_weights.astype(jnp.float32)

    def holder_step(carried, holder_index):
        numer_all, denom_all = carried
        row_start = (holder_index * STRIP).astype(jnp.int32)
        noise_win = lax.dynamic_slice_in_dim(noise_pad, row_start, PATCH, 2)
        cond_win = lax.dynamic_slice_in_dim(cond_pad, row_start, PATCH, 1)
        numer_win = lax.dynamic_slice_in_dim(numer_all, row_start, PATCH, 2)
        denom_win = lax.dynamic_slice_in_dim(denom_all, row_start, PATCH, 0)
        for slot_index in range(SLOTS):
            column = anchors[holder_index, slot_index].astype(jnp.int32)
            live_flag = slot_index < counts[holder_index]

            def compute_patch(unused_arg):
                noise_patch = lax.dynamic_slice_in_dim(noise_win, column, PATCH, 3)[None]
                cond_patch = lax.dynamic_slice_in_dim(cond_win, column, PATCH, 2)[None]
                return denoise(noise_patch, cond_patch, denoise_lift, denoise_conv, denoise_head)[0]

            def zero_patch(unused_arg):
                return jnp.zeros((MEMBERS, CH, PATCH, PATCH), jnp.float32)
            result = lax.cond(live_flag, compute_patch, zero_patch, 0)
            weight = weight_tile * live_flag.astype(jnp.float32)
            previous = lax.dynamic_slice_in_dim(numer_win, column, PATCH, 3)
            numer_win = lax.dynamic_update_slice_in_dim(numer_win, previous + weight * result, column, 3)
            previous_den = lax.dynamic_slice_in_dim(denom_win, column, PATCH, 1)
            denom_win = lax.dynamic_update_slice_in_dim(denom_win, previous_den + weight, column, 1)
        numer_all = lax.dynamic_update_slice_in_dim(numer_all, numer_win, row_start, 2)
        denom_all = lax.dynamic_update_slice_in_dim(denom_all, denom_win, row_start, 0)
        return ((numer_all, denom_all), 0)
    initial = (jnp.zeros((MEMBERS, CH, ROWS + PATCH, COLS), jnp.float32), jnp.zeros((ROWS + PATCH, COLS), jnp.float32))
    sums_out, unused_out = lax.scan(holder_step, initial, jnp.arange(N_TILE, dtype=jnp.int32))
    numer_dom = sums_out[0][:, :, :ROWS]
    denom_dom = sums_out[1][:ROWS]
    members = reg_mean[None] + numer_dom / jnp.maximum(denom_dom, 1.0)[None, None]
    ens_mean = lax.optimization_barrier(jnp.mean(members, axis=0))
    ens_var = lax.optimization_barrier(jnp.mean((members - ens_mean[None]) ** 2, axis=0))
    return (ens_mean, ens_var)
```

```python
import functools
import math

import jax
import jax.numpy as jnp
from jax import lax
from jax.experimental import pallas as pl
from jax.experimental.pallas import tpu as pltpu
from jax.sharding import PartitionSpec as P

POOL = 4
PAIR = 2 * POOL

skip_gain = 0.2
out_gain = 0.5 / math.sqrt(1.25)
in_gain = 1.0 / math.sqrt(1.25)

BF16 = jnp.bfloat16
F32 = jnp.float32
NN = (((1,), (0,)), ((), ()))
NT = (((1,), (1,)), ((), ()))
TN = (((0,), (0,)), ((), ()))


def mxu(lhs, rhs, dims=NN):
    return lax.dot_general(lhs, rhs, dims, preferred_element_type=F32)


def iota(shape, axis):
    return lax.broadcasted_iota(jnp.int32, shape, axis)


def one_hot(shape, rule):
    return jnp.where(rule(iota(shape, 0), iota(shape, 1)), 1.0, 0.0).astype(BF16)


def pool_rows(cells):
    cols = cells.shape[2]
    cells = cells + pltpu.roll(cells, PAIR - 1, 1)
    cells = cells + pltpu.roll(cells, PAIR - 2, 1)
    cells = cells + pltpu.roll(cells, cols - 1, 2)
    cells = cells + pltpu.roll(cells, cols - 2, 2)
    return (cells * (1.0 / (POOL * POOL))).reshape(-1, cols).astype(BF16)


def squeeze_of(channels):
    return one_hot((2 * channels, PAIR * channels), lambda r, c: c == POOL * r)


def build_taps(conv_ref, taps_ref):
    width = conv_ref.shape[2]
    for layer in range(conv_ref.shape[0]):
        for tap in range(3):
            for row_in in range(4):
                for row_out in range(2):
                    at = row_in - row_out
                    rows = pl.ds((tap * 4 + row_in) * width, width)
                    block = jnp.zeros((width, width), BF16)
                    if 0 <= at < 3:
                        block = conv_ref[layer, 3 * at + tap]
                    taps_ref[layer, rows, row_out * width : (row_out + 1) * width] = block


def shifts(cells, span):
    total, lanes = cells.shape
    column = iota((total, lanes), 0) % span
    left = jnp.where(column == 0, 0.0, pltpu.roll(cells, 1, 0))
    right = jnp.where(column == span - 1, 0.0, pltpu.roll(cells, total - 1, 0))
    return [left.astype(BF16), cells.astype(BF16), right.astype(BF16)]


def residual_pairs(parts, taps, stride):
    total, lanes = parts[0].shape
    count = total - stride
    half = lanes // 2
    lhs = jnp.concatenate([piece for part in parts for piece in (part[:count], part[stride:])], axis=1)
    term = mxu(lhs, taps)
    center = jnp.concatenate([parts[1][:count, half:], parts[1][stride:, :half]], axis=1)
    term = center.astype(F32) + term * jax.nn.sigmoid(term)
    return term.astype(BF16)


def edge_kernel(
    span,
    coarse_ref,
    noise_ref,
    table_ref,
    lift_ref,
    conv_ref,
    head_ref,
    nlow_ref,
    clow_ref,
    mean_ref,
    tables_ref,
    halo_ref,
    taps_ref,
    send_sem,
    recv_sem,
):
    channels, strip_rows, col_total = coarse_ref.shape
    width = lift_ref.shape[1]
    block_cols = col_total // POOL
    block_rows = strip_rows // POOL
    mine = lax.axis_index("tile")
    count = lax.axis_size("tile")
    barrier = pltpu.get_barrier_semaphore()

    def holds(place):
        return jnp.logical_and(place >= 0, place < count)

    moves = [
        (coarse_ref, halo_ref.at[0], 1),
        (coarse_ref, halo_ref.at[1], -1),
        (nlow_ref.at[2], nlow_ref.at[0], 1),
        (nlow_ref.at[1], nlow_ref.at[3], -1),
    ]
    moves = moves + [(table_ref.at[0], tables_ref.at[at], at) for at in range(span - 1, 0, -1)]
    steps = sorted({move[2] for move in moves})
    for step in steps:
        pl.semaphore_signal(
            barrier,
            inc=1,
            device_id={"tile": lax.rem(mine - step + count, count)},
            device_id_type=pl.DeviceIdType.MESH,
        )

    def copy_of(index):
        source, target, step = moves[index]
        return pltpu.make_async_remote_copy(
            src_ref=source,
            dst_ref=target,
            send_sem=send_sem.at[index],
            recv_sem=recv_sem.at[index],
            device_id={"tile": mine + step},
            device_id_type=pl.DeviceIdType.MESH,
        )

    def start(index):
        @pl.when(holds(mine + moves[index][2]))
        def _():
            copy_of(index).start()

    def finish(index):
        step = moves[index][2]

        @pl.when(holds(mine - step))
        def _():
            copy_of(index).wait_recv()

        @pl.when(holds(mine + step))
        def _():
            copy_of(index).wait_send()

    def clear(index):
        target, step = moves[index][1:]

        @pl.when(jnp.logical_not(holds(mine - step)))
        def _():
            target[...] = jnp.zeros(target.shape, target.dtype)

    pl.semaphore_wait(barrier, len(steps))
    for index in [0, 1] + list(range(4, len(moves))):
        start(index)
    noise = noise_ref[...].astype(F32)
    narrow = squeeze_of(2 * channels)
    for pair in range(2):
        low = pool_rows(noise[:, pair * PAIR : (pair + 1) * PAIR])
        nlow_ref[1 + pair] = mxu(narrow, low).astype(BF16)
    for index in range(len(moves)):
        clear(index)
    tables_ref[0] = table_ref[0]
    build_taps(conv_ref, taps_ref)
    start(2)
    start(3)

    pick = one_hot((block_cols, col_total), lambda r, c: c == POOL * r)
    spread = one_hot((block_cols, col_total), lambda r, c: c // POOL == r)
    by_channel = one_hot((PAIR * channels, channels), lambda r, c: r // PAIR == c)
    lift_rows = mxu(by_channel, lift_ref[...])
    at_row = iota(lift_rows.shape, 0) % PAIR
    lift_pair = jnp.concatenate(
        [jnp.where(at_row == 0, lift_rows, 0.0), jnp.where(at_row == POOL, lift_rows, 0.0)], axis=1
    ).astype(BF16)
    head_rows = mxu(by_channel, head_ref[...], NT)
    head_pair = jnp.concatenate(
        [jnp.where(at_row < POOL, head_rows, 0.0), jnp.where(at_row >= POOL, head_rows, 0.0)], axis=1
    ).astype(BF16)

    def lows_of(cells):
        cells = cells.astype(F32)
        return [pool_rows(cells[:, pair * PAIR : (pair + 1) * PAIR]) for pair in range(2)]

    def lifted(low):
        return mxu(mxu(pick, low, NT).astype(BF16), lift_pair).astype(BF16)

    own_low = lows_of(coarse_ref[...])
    own_act = [lifted(low) for low in own_low]
    finish(0)
    finish(1)
    above = halo_ref[0]
    below = halo_ref[1]
    above_low = lows_of(above)
    below_low = lows_of(below)
    acts = [lifted(low) for low in above_low] + own_act + [lifted(low) for low in below_low]
    hidden_act = jnp.concatenate(acts, axis=0).astype(F32)
    first_row = mine * block_rows - block_rows
    domain_rows = count * block_rows
    for layer in range(conv_ref.shape[0]):
        hidden_act = residual_pairs(shifts(hidden_act, block_cols), taps_ref[layer], block_cols)
        first_row = first_row + 1
        shape = hidden_act.shape
        rows = first_row + 2 * (iota(shape, 0) // block_cols) + iota(shape, 1) // width
        hidden_act = jnp.where(holds_rows(rows, domain_rows), hidden_act.astype(F32), 0.0)
    hidden_act = hidden_act.astype(BF16)

    fields = [above[:, PAIR:], coarse_ref[:, :PAIR], coarse_ref[:, PAIR:], below[:, :PAIR]]
    lows = [above_low[1]] + own_low + [below_low[0]]
    for pair in range(4):
        act = hidden_act[pair * block_cols : (pair + 1) * block_cols]
        rest = mxu(head_pair, act, NT)
        wide = 0.0
        for _ in range(3):
            part = rest.astype(BF16)
            wide = wide + mxu(part, spread)
            rest = rest - part.astype(F32)
        mean = fields[pair].astype(F32) + wide.reshape(channels, PAIR, col_total)
        if 1 <= pair <= 2:
            mean_ref[:, (pair - 1) * PAIR : pair * PAIR] = mean
        low = pool_rows(mean.astype(BF16).astype(F32))
        low = jnp.concatenate([low, lows[pair]], axis=0)
        clow_ref[pair] = mxu(narrow, low).astype(BF16)
    for index in range(2, len(moves)):
        finish(index)


def holds_rows(rows, domain_rows):
    return jnp.logical_and(rows >= 0, rows < domain_rows)


def edge(coarse, noise, table, lift, conv, head, span):
    channels, strip_rows, col_total = coarse.shape
    layers, _, width, _ = conv.shape
    vmem = pl.BlockSpec(memory_space=pltpu.VMEM)
    copies = span + 3
    return pl.pallas_call(
        functools.partial(edge_kernel, span),
        out_shape=(
            jax.ShapeDtypeStruct((4, 4 * channels, col_total), BF16),
            jax.ShapeDtypeStruct((4, 4 * channels, col_total), BF16),
            jax.ShapeDtypeStruct(coarse.shape, F32),
            jax.ShapeDtypeStruct((span, 1, 128), jnp.int32),
        ),
        in_specs=[vmem] * 6,
        out_specs=(vmem,) * 4,
        scratch_shapes=[
            pltpu.VMEM((2,) + coarse.shape, BF16),
            pltpu.VMEM((layers, 12 * width, 2 * width), BF16),
            pltpu.SemaphoreType.DMA((copies,)),
            pltpu.SemaphoreType.DMA((copies,)),
        ],
        compiler_params=pltpu.CompilerParams(collective_id=0, has_side_effects=True),
        name="edge",
    )(coarse, noise, table, lift, conv, head)


def patch_kernel(
    slot_total,
    table_ref,
    nlow_ref,
    clow_ref,
    mean_ref,
    noise_ref,
    weight_ref,
    lift_ref,
    conv_ref,
    head_ref,
    out_mean_ref,
    out_var_ref,
    taps_ref,
    field_ref,
    wide_ref,
    acc_ref,
    den_ref,
):
    feat_rows, strip_rows, col_total = noise_ref.shape
    channels = mean_ref.shape[0]
    members = feat_rows // channels
    width = lift_ref.shape[1]
    patch = weight_ref.shape[0]
    span = patch // strip_rows
    block_cols = patch // POOL
    offsets = col_total // POOL
    pad = 8

    build_taps(conv_ref, taps_ref)
    acc_ref[...] = jnp.zeros_like(acc_ref)
    den_ref[...] = jnp.zeros_like(den_ref)
    wide_ref[...] = jnp.zeros_like(wide_ref)
    wide_ref[:, :patch] = weight_ref[...].astype(F32)

    low_rows = 2 * feat_rows + 4 * channels
    noise_rows = 2 * feat_rows

    def source(row, column):
        noise_at = (row // 2) % channels
        cond_at = channels + (row - noise_rows) // 2
        return column == jnp.where(row < noise_rows, noise_at, cond_at)

    base = mxu(one_hot((low_rows, 3 * channels), source), lift_ref[...])
    row = iota(base.shape, 0)
    blocks = []
    for member in range(members):
        first = 2 * channels * member
        for half in range(2):
            keep = (row >= first) & (row < first + 2 * channels) & (row % 2 == half)
            blocks.append(jnp.where(keep, base, 0.0))
    noise_lift = jnp.concatenate(blocks, axis=1).astype(BF16)
    cond_lift = jnp.concatenate(
        [jnp.where((row >= noise_rows) & (row % 2 == half), base, 0.0) for half in range(2)], axis=1
    ).astype(BF16)
    order = one_hot((col_total, col_total), lambda r, c: c == POOL * (r % offsets) + r // offsets)
    for pair in range(4):
        low = jnp.concatenate([nlow_ref[pair], clow_ref[pair]], axis=0)
        turned = mxu(order, low, NT).astype(BF16)
        cond = mxu(turned, cond_lift)
        act = in_gain * mxu(turned, noise_lift) + jnp.concatenate([cond] * members, axis=1)
        act = act.astype(BF16).astype(F32)
        for phase in range(POOL):
            for member in range(members):
                for half in range(2):
                    first = (member * 2 + half) * width
                    field_ref[phase, pair * members + member, half, pad : pad + offsets] = act[
                        phase * offsets : (phase + 1) * offsets, first : first + width
                    ]

    lanes = 128
    head_wide = one_hot((channels, lanes), lambda r, c: (c % channels == r) & (c < 4 * feat_rows))
    head_wide = mxu(head_ref[...], head_wide)
    lane = iota(head_wide.shape, 1)
    heads = []
    for pair in range(2):
        for member in range(members):
            for half in range(2):
                first = (2 * pair + half) * feat_rows + member * channels
                keep = (lane >= first) & (lane < first + channels)
                heads.append(jnp.where(keep, head_wide, 0.0))
    heads = jnp.concatenate(heads, axis=0).astype(BF16)

    stride = members * block_cols

    def step(index, carry):
        offset = index // slot_total
        slot = index - offset * slot_total
        column = table_ref[offset, 0, slot]
        live = slot < table_ref[offset, 0, slot_total]

        @pl.when(live)
        def _():
            phase = column & (POOL - 1)
            start = (column >> 2) + pad
            is_top = offset == 0
            is_bottom = offset == span - 1
            cell = iota((block_cols, 2 * width), 0)
            parts = []
            for tap in range(3):
                rows = []
                for pair in range(4):
                    for member in range(members):
                        which = pair * members + member
                        window = pl.ds(start + tap - 1, block_cols)
                        at = jnp.concatenate([field_ref[phase, which, half, window, :] for half in range(2)], axis=1)
                        if tap == 0:
                            at = jnp.where(cell == 0, 0.0, at)
                        if tap == 2:
                            at = jnp.where(cell == block_cols - 1, 0.0, at)
                        if pair == 0:
                            at = jnp.where(is_top, 0.0, at)
                        if pair == 3:
                            at = jnp.where(is_bottom, 0.0, at)
                        rows.append(at)
                parts.append(jnp.concatenate(rows, axis=0).astype(BF16))
            act = residual_pairs(parts, taps_ref[0], stride).astype(F32)
            side = iota((stride, 2 * width), 1) // width
            top = jnp.where(jnp.logical_and(is_top, side == 0), 0.0, act[:stride])
            bottom = jnp.where(jnp.logical_and(is_bottom, side == 1), 0.0, act[2 * stride :])
            act = jnp.concatenate([top, act[stride : 2 * stride], bottom], axis=0)
            act = residual_pairs(shifts(act, block_cols), taps_ref[1], stride).astype(F32)
            act = jnp.concatenate(
                [act[at * block_cols : (at + 1) * block_cols] for at in range(2 * members)], axis=1
            ).astype(BF16)
            term = mxu(act, heads)
            high = term.astype(BF16)
            low = (term - high.astype(F32)).astype(BF16)
            cols = iota((block_cols, col_total), 1)
            blocks = iota((block_cols, col_total), 0)
            place = jnp.where(((cols - column) >> 2) == blocks, 1.0, 0.0).astype(BF16)
            placed = mxu(high, place, TN) + mxu(low, place, TN)
            first = pl.multiple_of(offset * strip_rows, strip_rows)
            weights = pltpu.roll(wide_ref[pl.ds(first, strip_rows), :], column, axis=1)
            den_ref[...] += weights
            for at in range(strip_rows):
                below = (at // POOL) * feat_rows
                acc_ref[at] += weights[at : at + 1, :] * placed[below : below + feat_rows, :]

        return carry

    lax.fori_loop(0, span * slot_total, step, 0)

    denom = den_ref[...]
    scale = 1.0 / jnp.maximum(denom, 1.0)
    for channel in range(channels):
        outs = []
        for member in range(members):
            at = member * channels + channel
            numer = skip_gain * noise_ref[at].astype(F32) * denom + out_gain * acc_ref[:, at, :]
            outs.append(mean_ref[channel] + numer * scale)
        ens_mean = sum(outs) * (1.0 / members)
        out_mean_ref[channel] = ens_mean
        out_var_ref[channel] = sum((out - ens_mean) ** 2 for out in outs) * (1.0 / members)


def patches(tables, nlow, clow, mean, noise, weights, lift, conv, head, slot_total):
    feat_rows, strip_rows, col_total = noise.shape
    layers, _, width, _ = conv.shape
    members = feat_rows // mean.shape[0]
    vmem = pl.BlockSpec(memory_space=pltpu.VMEM)
    return pl.pallas_call(
        functools.partial(patch_kernel, slot_total),
        out_shape=(jax.ShapeDtypeStruct(mean.shape, F32),) * 2,
        in_specs=[pl.BlockSpec(memory_space=pltpu.SMEM)] + [vmem] * 8,
        out_specs=(vmem, vmem),
        scratch_shapes=[
            pltpu.VMEM((layers, 12 * width, 2 * width), BF16),
            pltpu.VMEM((POOL, 4 * members, 2, col_total // POOL + 16, width), F32),
            pltpu.VMEM((weights.shape[0], col_total), F32),
            pltpu.VMEM((strip_rows, feat_rows, col_total), F32),
            pltpu.VMEM((strip_rows, col_total), F32),
        ],
        name="patches",
    )(tables, nlow, clow, mean, noise, weights, lift, conv, head)


def local(
    coarse,
    noise_field,
    anchors,
    counts,
    blend_weights,
    regress_lift,
    regress_conv,
    regress_head,
    denoise_lift,
    denoise_conv,
    denoise_head,
):
    members, channels, strip_rows, col_total = noise_field.shape
    span = blend_weights.shape[0] // strip_rows
    slot_total = anchors.shape[1]
    noise = noise_field.reshape(members * channels, strip_rows, col_total)
    table = jnp.concatenate([anchors, counts[:, None]], axis=1)
    table = jnp.pad(table, ((0, 0), (0, 127 - slot_total)))[None]
    nlow, clow, mean, tables = edge(coarse, noise, table, regress_lift, regress_conv, regress_head, span)
    return patches(
        tables, nlow, clow, mean, noise, blend_weights, denoise_lift, denoise_conv, denoise_head, slot_total
    )


def solution(mesh):
    in_specs = (
        P(None, ("groups", "tile"), None),
        P(None, None, ("groups", "tile"), None),
        P(("groups", "tile"), None),
        P(("groups", "tile")),
        P(),
        P(),
        P(),
        P(),
        P(),
        P(),
        P(),
    )
    out_specs = (P(None, ("groups", "tile"), None), P(None, ("groups", "tile"), None))
    return jax.shard_map(local, mesh=mesh, in_specs=in_specs, out_specs=out_specs, check_vma=False)
```

```python
import functools
import math

import jax
import jax.numpy as jnp
from jax import lax
from jax.experimental import pallas as pl
from jax.experimental.pallas import tpu as pltpu
from jax.sharding import PartitionSpec as P

POOL = 4
PAIR = 2 * POOL
GROUP = 2

skip_gain = 0.2
out_gain = 0.5 / math.sqrt(1.25)
in_gain = 1.0 / math.sqrt(1.25)

BF16 = jnp.bfloat16
F32 = jnp.float32
NN = (((1,), (0,)), ((), ()))
NT = (((1,), (1,)), ((), ()))
TN = (((0,), (0,)), ((), ()))


def mxu(lhs, rhs, dims=NN):
    return lax.dot_general(lhs, rhs, dims, preferred_element_type=F32)


def iota(shape, axis):
    return lax.broadcasted_iota(jnp.int32, shape, axis)


def one_hot(shape, rule):
    return jnp.where(rule(iota(shape, 0), iota(shape, 1)), 1.0, 0.0).astype(BF16)


def pool_rows(cells):
    cols = cells.shape[2]
    cells = cells + pltpu.roll(cells, PAIR - 1, 1)
    cells = cells + pltpu.roll(cells, PAIR - 2, 1)
    cells = cells + pltpu.roll(cells, cols - 1, 2)
    cells = cells + pltpu.roll(cells, cols - 2, 2)
    return (cells * (1.0 / (POOL * POOL))).reshape(-1, cols).astype(BF16)


def squeeze_of(channels):
    return one_hot((2 * channels, PAIR * channels), lambda r, c: c == POOL * r)


def build_taps(conv_ref, taps_ref):
    width = conv_ref.shape[2]
    for layer in range(conv_ref.shape[0]):
        for tap in range(3):
            for row_in in range(4):
                for row_out in range(2):
                    at = row_in - row_out
                    rows = pl.ds((tap * 4 + row_in) * width, width)
                    block = jnp.zeros((width, width), BF16)
                    if 0 <= at < 3:
                        block = conv_ref[layer, 3 * at + tap]
                    taps_ref[layer, rows, row_out * width : (row_out + 1) * width] = block


def shifts(cells, span):
    total, lanes = cells.shape
    column = iota((total, lanes), 0) % span
    left = jnp.where(column == 0, 0.0, pltpu.roll(cells, 1, 0))
    right = jnp.where(column == span - 1, 0.0, pltpu.roll(cells, total - 1, 0))
    return [left.astype(BF16), cells.astype(BF16), right.astype(BF16)]


def residual_pairs(parts, taps, stride):
    total, lanes = parts[0].shape
    count = total - stride
    half = lanes // 2
    lhs = jnp.concatenate([piece for part in parts for piece in (part[:count], part[stride:])], axis=1)
    term = mxu(lhs, taps)
    center = jnp.concatenate([parts[1][:count, half:], parts[1][stride:, :half]], axis=1)
    term = center.astype(F32) + term * jax.nn.sigmoid(term)
    return term.astype(BF16)


def edge_kernel(
    span,
    coarse_ref,
    noise_ref,
    table_ref,
    lift_ref,
    conv_ref,
    head_ref,
    nlow_ref,
    clow_ref,
    mean_ref,
    tables_ref,
    halo_ref,
    taps_ref,
    send_sem,
    recv_sem,
):
    channels, strip_rows, col_total = coarse_ref.shape
    width = lift_ref.shape[1]
    block_cols = col_total // POOL
    block_rows = strip_rows // POOL
    mine = lax.axis_index("tile")
    count = lax.axis_size("tile")
    barrier = pltpu.get_barrier_semaphore()

    def holds(place):
        return jnp.logical_and(place >= 0, place < count)

    moves = [
        (coarse_ref, halo_ref.at[0], 1),
        (coarse_ref, halo_ref.at[1], -1),
        (nlow_ref.at[2], nlow_ref.at[0], 1),
        (nlow_ref.at[1], nlow_ref.at[3], -1),
    ]
    moves = moves + [(table_ref.at[0], tables_ref.at[at], at) for at in range(span - 1, 0, -1)]
    steps = sorted({move[2] for move in moves})
    for step in steps:
        pl.semaphore_signal(
            barrier,
            inc=1,
            device_id={"tile": lax.rem(mine - step + count, count)},
            device_id_type=pl.DeviceIdType.MESH,
        )

    def copy_of(index):
        source, target, step = moves[index]
        return pltpu.make_async_remote_copy(
            src_ref=source,
            dst_ref=target,
            send_sem=send_sem.at[index],
            recv_sem=recv_sem.at[index],
            device_id={"tile": mine + step},
            device_id_type=pl.DeviceIdType.MESH,
        )

    def start(index):
        @pl.when(holds(mine + moves[index][2]))
        def _():
            copy_of(index).start()

    def finish(index):
        step = moves[index][2]

        @pl.when(holds(mine - step))
        def _():
            copy_of(index).wait_recv()

        @pl.when(holds(mine + step))
        def _():
            copy_of(index).wait_send()

    def clear(index):
        target, step = moves[index][1:]

        @pl.when(jnp.logical_not(holds(mine - step)))
        def _():
            target[...] = jnp.zeros(target.shape, target.dtype)

    pl.semaphore_wait(barrier, len(steps))
    for index in [0, 1] + list(range(4, len(moves))):
        start(index)
    noise = noise_ref[...].astype(F32)
    narrow = squeeze_of(2 * channels)
    for pair in range(2):
        low = pool_rows(noise[:, pair * PAIR : (pair + 1) * PAIR])
        nlow_ref[1 + pair] = mxu(narrow, low).astype(BF16)
    for index in range(len(moves)):
        clear(index)
    tables_ref[0] = table_ref[0]
    build_taps(conv_ref, taps_ref)
    start(2)
    start(3)

    pick = one_hot((block_cols, col_total), lambda r, c: c == POOL * r)
    spread = one_hot((block_cols, col_total), lambda r, c: c // POOL == r)
    by_channel = one_hot((PAIR * channels, channels), lambda r, c: r // PAIR == c)
    lift_rows = mxu(by_channel, lift_ref[...])
    at_row = iota(lift_rows.shape, 0) % PAIR
    lift_pair = jnp.concatenate(
        [jnp.where(at_row == 0, lift_rows, 0.0), jnp.where(at_row == POOL, lift_rows, 0.0)], axis=1
    ).astype(BF16)
    head_rows = mxu(by_channel, head_ref[...], NT)
    head_pair = jnp.concatenate(
        [jnp.where(at_row < POOL, head_rows, 0.0), jnp.where(at_row >= POOL, head_rows, 0.0)], axis=1
    ).astype(BF16)

    def lows_of(cells):
        cells = cells.astype(F32)
        return [pool_rows(cells[:, pair * PAIR : (pair + 1) * PAIR]) for pair in range(2)]

    def lifted(low):
        return mxu(mxu(pick, low, NT).astype(BF16), lift_pair).astype(BF16)

    own_low = lows_of(coarse_ref[...])
    own_act = [lifted(low) for low in own_low]
    finish(0)
    finish(1)
    above = halo_ref[0]
    below = halo_ref[1]
    above_low = lows_of(above)
    below_low = lows_of(below)
    acts = [lifted(low) for low in above_low] + own_act + [lifted(low) for low in below_low]
    hidden_act = jnp.concatenate(acts, axis=0).astype(F32)
    first_row = mine * block_rows - block_rows
    domain_rows = count * block_rows
    for layer in range(conv_ref.shape[0]):
        hidden_act = residual_pairs(shifts(hidden_act, block_cols), taps_ref[layer], block_cols)
        first_row = first_row + 1
        shape = hidden_act.shape
        rows = first_row + 2 * (iota(shape, 0) // block_cols) + iota(shape, 1) // width
        hidden_act = jnp.where(holds_rows(rows, domain_rows), hidden_act.astype(F32), 0.0)
    hidden_act = hidden_act.astype(BF16)

    fields = [above[:, PAIR:], coarse_ref[:, :PAIR], coarse_ref[:, PAIR:], below[:, :PAIR]]
    lows = [above_low[1]] + own_low + [below_low[0]]
    for pair in range(4):
        act = hidden_act[pair * block_cols : (pair + 1) * block_cols]
        rest = mxu(head_pair, act, NT)
        wide = 0.0
        for _ in range(3):
            part = rest.astype(BF16)
            wide = wide + mxu(part, spread)
            rest = rest - part.astype(F32)
        mean = fields[pair].astype(F32) + wide.reshape(channels, PAIR, col_total)
        if 1 <= pair <= 2:
            mean_ref[:, (pair - 1) * PAIR : pair * PAIR] = mean
        low = pool_rows(mean.astype(BF16).astype(F32))
        low = jnp.concatenate([low, lows[pair]], axis=0)
        clow_ref[pair] = mxu(narrow, low).astype(BF16)
    for index in range(2, len(moves)):
        finish(index)


def holds_rows(rows, domain_rows):
    return jnp.logical_and(rows >= 0, rows < domain_rows)


def edge(coarse, noise, table, lift, conv, head, span):
    channels, strip_rows, col_total = coarse.shape
    layers, _, width, _ = conv.shape
    vmem = pl.BlockSpec(memory_space=pltpu.VMEM)
    copies = span + 3
    return pl.pallas_call(
        functools.partial(edge_kernel, span),
        out_shape=(
            jax.ShapeDtypeStruct((4, 4 * channels, col_total), BF16),
            jax.ShapeDtypeStruct((4, 4 * channels, col_total), BF16),
            jax.ShapeDtypeStruct(coarse.shape, F32),
            jax.ShapeDtypeStruct((span, 1, 128), jnp.int32),
        ),
        in_specs=[vmem] * 6,
        out_specs=(vmem,) * 4,
        scratch_shapes=[
            pltpu.VMEM((2,) + coarse.shape, BF16),
            pltpu.VMEM((layers, 12 * width, 2 * width), BF16),
            pltpu.SemaphoreType.DMA((copies,)),
            pltpu.SemaphoreType.DMA((copies,)),
        ],
        compiler_params=pltpu.CompilerParams(collective_id=0, has_side_effects=True),
        name="edge",
    )(coarse, noise, table, lift, conv, head)


def patch_kernel(
    slot_total,
    table_ref,
    nlow_ref,
    clow_ref,
    mean_ref,
    noise_ref,
    weight_ref,
    lift_ref,
    conv_ref,
    head_ref,
    out_mean_ref,
    out_var_ref,
    taps_ref,
    field_ref,
    wide_ref,
    acc_ref,
    den_ref,
    stage_ref,
    list_ref,
):
    feat_rows, strip_rows, col_total = noise_ref.shape
    channels = mean_ref.shape[0]
    members = feat_rows // channels
    width = lift_ref.shape[1]
    patch = weight_ref.shape[0]
    span = patch // strip_rows
    block_cols = patch // POOL
    offsets = col_total // POOL
    pad = 8

    build_taps(conv_ref, taps_ref)
    acc_ref[...] = jnp.zeros_like(acc_ref)
    den_ref[...] = jnp.zeros_like(den_ref)
    wide_ref[...] = jnp.zeros_like(wide_ref)
    wide_ref[:, :patch] = weight_ref[...].astype(F32)

    low_rows = 2 * feat_rows + 4 * channels
    noise_rows = 2 * feat_rows

    def source(row, column):
        noise_at = (row // 2) % channels
        cond_at = channels + (row - noise_rows) // 2
        return column == jnp.where(row < noise_rows, noise_at, cond_at)

    base = mxu(one_hot((low_rows, 3 * channels), source), lift_ref[...])
    row = iota(base.shape, 0)
    blocks = []
    for member in range(members):
        first = 2 * channels * member
        for half in range(2):
            keep = (row >= first) & (row < first + 2 * channels) & (row % 2 == half)
            blocks.append(jnp.where(keep, base, 0.0))
    noise_lift = jnp.concatenate(blocks, axis=1).astype(BF16)
    cond_lift = jnp.concatenate(
        [jnp.where((row >= noise_rows) & (row % 2 == half), base, 0.0) for half in range(2)], axis=1
    ).astype(BF16)
    order = one_hot((col_total, col_total), lambda r, c: c == POOL * (r % offsets) + r // offsets)
    for pair in range(4):
        low = jnp.concatenate([nlow_ref[pair], clow_ref[pair]], axis=0)
        turned = mxu(order, low, NT).astype(BF16)
        cond = mxu(turned, cond_lift)
        act = in_gain * mxu(turned, noise_lift) + jnp.concatenate([cond] * members, axis=1)
        act = act.astype(BF16).astype(F32)
        for phase in range(POOL):
            for member in range(members):
                for half in range(2):
                    first = (member * 2 + half) * width
                    field_ref[phase, pair * members + member, half, pad : pad + offsets] = act[
                        phase * offsets : (phase + 1) * offsets, first : first + width
                    ]

    lanes = 128
    head_wide = one_hot((channels, lanes), lambda r, c: (c % channels == r) & (c < 4 * feat_rows))
    head_wide = mxu(head_ref[...], head_wide)
    lane = iota(head_wide.shape, 1)
    heads = []
    for pair in range(2):
        for member in range(members):
            for half in range(2):
                first = (2 * pair + half) * feat_rows + member * channels
                keep = (lane >= first) & (lane < first + channels)
                heads.append(jnp.where(keep, head_wide, 0.0))
    heads = jnp.concatenate(heads, axis=0).astype(BF16)

    group = stage_ref.shape[1]
    slots = 4 * members
    stage_ref[...] = jnp.zeros_like(stage_ref)
    field_ref[:, slots] = jnp.zeros(field_ref.shape[:1] + field_ref.shape[2:], F32)
    stride = group * members * block_cols
    reach = 3 * lanes

    def note(index, found):
        offset = index // slot_total
        slot = index - offset * slot_total
        live = slot < table_ref[offset, 0, slot_total]

        @pl.when(live)
        def _():
            list_ref[found] = index

        return found + live.astype(jnp.int32)

    def blank(index, carry):
        list_ref[index] = 0
        return carry

    lax.fori_loop(0, list_ref.shape[0], blank, 0)
    live_total = lax.fori_loop(0, span * slot_total, note, 0)

    def step(turn, carry):
        pieces = []
        for at in range(group):
            place = turn * group + at
            index = list_ref[place]
            offset = index // slot_total
            column = table_ref[offset, 0, index - offset * slot_total]
            pieces.append((offset, column, place < live_total))
        edge_cell = iota((8, width), 0)
        parts = []
        for tap in range(3):
            sides = []
            for half in range(2):
                rows = []
                for pair in range(4):
                    for offset, column, _ in pieces:
                        phase = column & (POOL - 1)
                        window = pl.ds((column >> 2) + pad + tap - 1, block_cols)
                        for member in range(members):
                            which = pair * members + member
                            if pair == 0:
                                which = jnp.where(offset == 0, slots, which)
                            if pair == 3:
                                which = jnp.where(offset == span - 1, slots, which)
                            at = field_ref[phase, which, half, window, :]
                            if tap == 0:
                                at = jnp.concatenate([jnp.where(edge_cell == 0, 0.0, at[:8]), at[8:]], axis=0)
                            if tap == 2:
                                at = jnp.concatenate([at[:-8], jnp.where(edge_cell == 7, 0.0, at[-8:])], axis=0)
                            rows.append(at)
                sides.append(jnp.concatenate(rows, axis=0))
            parts.append(jnp.concatenate(sides, axis=1).astype(BF16))
        act = residual_pairs(parts, taps_ref[0], stride).astype(F32)
        parts = [[], [], []]
        for half in range(2):
            rows = [[], [], []]
            for pair in range(3):
                for at, (offset, _, _) in enumerate(pieces):
                    for member in range(members):
                        first = ((pair * group + at) * members + member) * block_cols
                        cells = act[first : first + block_cols, half * width : (half + 1) * width]
                        if pair == 0 and half == 0:
                            cells = jnp.where(offset == 0, 0.0, cells)
                        if pair == 2 and half == 1:
                            cells = jnp.where(offset == span - 1, 0.0, cells)
                        hold = stage_ref.at[half, at, pair * members + member]
                        hold[8 : 8 + block_cols] = cells
                        rows[0].append(hold[7 : 7 + block_cols])
                        rows[1].append(cells)
                        rows[2].append(hold[9 : 9 + block_cols])
            for tap in range(3):
                parts[tap].append(jnp.concatenate(rows[tap], axis=0))
        parts = [jnp.concatenate(sides, axis=1).astype(BF16) for sides in parts]
        act = residual_pairs(parts, taps_ref[1], stride).astype(F32)
        rows = []
        for at in range(group):
            sides = []
            for pair in range(2):
                for member in range(members):
                    first = ((pair * group + at) * members + member) * block_cols
                    sides.append(act[first : first + block_cols])
            rows.append(jnp.concatenate(sides, axis=1))
        terms = mxu(jnp.concatenate(rows, axis=0).astype(BF16), heads)
        cols = iota((block_cols, reach), 1)
        blocks = iota((block_cols, reach), 0)
        for at, (offset, column, live) in enumerate(pieces):
            term = terms[at * block_cols : (at + 1) * block_cols]
            high = term.astype(BF16)
            low = (term - high.astype(F32)).astype(BF16)
            first = jnp.minimum(column // lanes, col_total // lanes - 3) * lanes
            inner = column - first
            span_cols = pl.ds(pl.multiple_of(first, lanes), reach)
            place = jnp.where(((cols - inner) >> 2) == blocks, 1.0, 0.0).astype(BF16)
            placed = mxu(high, place, TN) + mxu(low, place, TN)
            top = pl.multiple_of(offset * strip_rows, strip_rows)
            weights = pltpu.roll(wide_ref[pl.ds(top, strip_rows), :], inner, axis=1)
            weights = jnp.where(live, weights, 0.0)
            den_ref[:, span_cols] += weights
            for row in range(strip_rows):
                below = (row // POOL) * feat_rows
                acc_ref[row, :, span_cols] += weights[row : row + 1, :] * placed[below : below + feat_rows, :]
        return carry

    lax.fori_loop(0, (live_total + group - 1) // group, step, 0)

    denom = den_ref[...]
    scale = 1.0 / jnp.maximum(denom, 1.0)
    for channel in range(channels):
        outs = []
        for member in range(members):
            at = member * channels + channel
            numer = skip_gain * noise_ref[at].astype(F32) * denom + out_gain * acc_ref[:, at, :]
            outs.append(mean_ref[channel] + numer * scale)
        ens_mean = sum(outs) * (1.0 / members)
        out_mean_ref[channel] = ens_mean
        out_var_ref[channel] = sum((out - ens_mean) ** 2 for out in outs) * (1.0 / members)


def patches(tables, nlow, clow, mean, noise, weights, lift, conv, head, slot_total):
    feat_rows, strip_rows, col_total = noise.shape
    layers, _, width, _ = conv.shape
    members = feat_rows // mean.shape[0]
    vmem = pl.BlockSpec(memory_space=pltpu.VMEM)
    return pl.pallas_call(
        functools.partial(patch_kernel, slot_total),
        out_shape=(jax.ShapeDtypeStruct(mean.shape, F32),) * 2,
        in_specs=[pl.BlockSpec(memory_space=pltpu.SMEM)] + [vmem] * 8,
        out_specs=(vmem, vmem),
        scratch_shapes=[
            pltpu.VMEM((layers, 12 * width, 2 * width), BF16),
            pltpu.VMEM((POOL, 4 * members + 1, 2, col_total // POOL + 16, width), F32),
            pltpu.VMEM((weights.shape[0], 3 * 128), F32),
            pltpu.VMEM((strip_rows, feat_rows, col_total), F32),
            pltpu.VMEM((strip_rows, col_total), F32),
            pltpu.VMEM((2, GROUP, 3 * members, weights.shape[0] // POOL + 16, width), F32),
            pltpu.SMEM((weights.shape[0] // strip_rows * slot_total + GROUP,), jnp.int32),
        ],
        name="patches",
    )(tables, nlow, clow, mean, noise, weights, lift, conv, head)


def local(
    coarse,
    noise_field,
    anchors,
    counts,
    blend_weights,
    regress_lift,
    regress_conv,
    regress_head,
    denoise_lift,
    denoise_conv,
    denoise_head,
):
    members, channels, strip_rows, col_total = noise_field.shape
    span = blend_weights.shape[0] // strip_rows
    slot_total = anchors.shape[1]
    noise = noise_field.reshape(members * channels, strip_rows, col_total)
    table = jnp.concatenate([anchors, counts[:, None]], axis=1)
    table = jnp.pad(table, ((0, 0), (0, 127 - slot_total)))[None]
    nlow, clow, mean, tables = edge(coarse, noise, table, regress_lift, regress_conv, regress_head, span)
    return patches(
        tables, nlow, clow, mean, noise, blend_weights, denoise_lift, denoise_conv, denoise_head, slot_total
    )


def solution(mesh):
    in_specs = (
        P(None, ("groups", "tile"), None),
        P(None, None, ("groups", "tile"), None),
        P(("groups", "tile"), None),
        P(("groups", "tile")),
        P(),
        P(),
        P(),
        P(),
        P(),
        P(),
        P(),
    )
    out_specs = (P(None, ("groups", "tile"), None), P(None, ("groups", "tile"), None))
    return jax.shard_map(local, mesh=mesh, in_specs=in_specs, out_specs=out_specs, check_vma=False)
```

```python
import functools
import math

import jax
import jax.numpy as jnp
from jax import lax
from jax.experimental import pallas as pl
from jax.experimental.pallas import tpu as pltpu
from jax.sharding import PartitionSpec as P

POOL = 4
PAIR = 2 * POOL
GROUP = 3

skip_gain = 0.2
out_gain = 0.5 / math.sqrt(1.25)
in_gain = 1.0 / math.sqrt(1.25)

BF16 = jnp.bfloat16
F32 = jnp.float32
NN = (((1,), (0,)), ((), ()))
NT = (((1,), (1,)), ((), ()))
TN = (((0,), (0,)), ((), ()))


def mxu(lhs, rhs, dims=NN):
    return lax.dot_general(lhs, rhs, dims, preferred_element_type=F32)


def iota(shape, axis):
    return lax.broadcasted_iota(jnp.int32, shape, axis)


def one_hot(shape, rule):
    return jnp.where(rule(iota(shape, 0), iota(shape, 1)), 1.0, 0.0).astype(BF16)


def pool_of(pairs, channels):
    depth = PAIR * pairs

    def rule(row, column):
        pair = row // (2 * channels)
        channel = row % (2 * channels) // 2
        block = 2 * pair + row % 2
        return (channel == column // depth) & (block == column % depth // POOL)

    return one_hot((2 * pairs * channels, depth * channels), rule)


def pooled(rule, cells):
    cols = cells.shape[-1]
    sums = mxu(rule, cells.reshape(-1, cols))
    sums = sums + pltpu.roll(sums, cols - 1, 1)
    sums = sums + pltpu.roll(sums, cols - 2, 1)
    return sums * (1.0 / (POOL * POOL))


def build_taps(conv_ref, taps_ref):
    width = conv_ref.shape[2]
    for layer in range(conv_ref.shape[0]):
        for tap in range(3):
            for row_in in range(4):
                for row_out in range(2):
                    at = row_in - row_out
                    rows = pl.ds((tap * 4 + row_in) * width, width)
                    block = jnp.zeros((width, width), BF16)
                    if 0 <= at < 3:
                        block = conv_ref[layer, 3 * at + tap]
                    if tap * 4 + row_in >= 6:
                        block = -block
                    taps_ref[layer, rows, row_out * width : (row_out + 1) * width] = block


def shifts(cells, holds):
    parts = [[], [], []]
    for half, runs in enumerate(cells):
        rows = [[], [], []]
        for at, run in enumerate(runs):
            count = run.shape[0]
            hold = holds(half, at)
            hold[8 : 8 + count] = run
            rows[0].append(hold[7 : 7 + count])
            rows[1].append(run)
            rows[2].append(hold[9 : 9 + count])
        for tap in range(3):
            parts[tap].append(jnp.concatenate(rows[tap], axis=0))
    return [jnp.concatenate(sides, axis=1).astype(BF16) for sides in parts]


def residual_pairs(parts, taps, stride):
    total, lanes = parts[0].shape
    count = total - stride
    half = lanes // 2
    pieces = [piece for part in parts for piece in (part[:count], part[stride:])]
    depth = taps.shape[0] // 2
    term = mxu(jnp.concatenate(pieces[:3], axis=1), taps[:depth])
    term = term - mxu(jnp.concatenate(pieces[3:], axis=1), taps[depth:])
    center = jnp.concatenate([parts[1][:count, half:], parts[1][stride:, :half]], axis=1)
    term = center.astype(F32) + term * jax.nn.sigmoid(term)
    return term.astype(BF16)


def edge_kernel(
    span,
    coarse_ref,
    noise_ref,
    table_ref,
    lift_ref,
    conv_ref,
    head_ref,
    nlow_ref,
    clow_ref,
    mean_ref,
    tables_ref,
    halo_ref,
    taps_ref,
    stage_ref,
    send_sem,
    recv_sem,
):
    channels, strip_rows, col_total = coarse_ref.shape
    width = lift_ref.shape[1]
    block_cols = col_total // POOL
    block_rows = strip_rows // POOL
    mine = lax.axis_index("tile")
    count = lax.axis_size("tile")
    barrier = pltpu.get_barrier_semaphore()

    def holds(place):
        return jnp.logical_and(place >= 0, place < count)

    moves = [
        (coarse_ref, halo_ref.at[0], 1),
        (coarse_ref, halo_ref.at[1], -1),
        (nlow_ref.at[2], nlow_ref.at[0], 1),
        (nlow_ref.at[1], nlow_ref.at[3], -1),
    ]
    moves = moves + [(table_ref.at[0], tables_ref.at[at], at) for at in range(span - 1, 0, -1)]
    steps = sorted({move[2] for move in moves})
    for step in steps:
        pl.semaphore_signal(
            barrier,
            inc=1,
            device_id={"tile": lax.rem(mine - step + count, count)},
            device_id_type=pl.DeviceIdType.MESH,
        )

    def copy_of(index):
        source, target, step = moves[index]
        return pltpu.make_async_remote_copy(
            src_ref=source,
            dst_ref=target,
            send_sem=send_sem.at[index],
            recv_sem=recv_sem.at[index],
            device_id={"tile": mine + step},
            device_id_type=pl.DeviceIdType.MESH,
        )

    def start(index):
        @pl.when(holds(mine + moves[index][2]))
        def _():
            copy_of(index).start()

    def finish(index):
        step = moves[index][2]

        @pl.when(holds(mine - step))
        def _():
            copy_of(index).wait_recv()

        @pl.when(holds(mine + step))
        def _():
            copy_of(index).wait_send()

    def clear(index):
        target, step = moves[index][1:]

        @pl.when(jnp.logical_not(holds(mine - step)))
        def _():
            target[...] = jnp.zeros(target.shape, target.dtype)

    pl.semaphore_wait(barrier, len(steps))
    for index in [0, 1] + list(range(4, len(moves))):
        start(index)
    low = pooled(pool_of(2, 2 * channels), noise_ref[...]).astype(BF16)
    for pair in range(2):
        nlow_ref[1 + pair] = low[pair * 4 * channels : (pair + 1) * 4 * channels]
    for index in range(len(moves)):
        clear(index)
    tables_ref[0] = table_ref[0]
    build_taps(conv_ref, taps_ref)
    start(2)
    start(3)

    pick = one_hot((block_cols, col_total), lambda r, c: c == POOL * r)
    spread = one_hot((block_cols, col_total), lambda r, c: c // POOL == r)
    lift_rows = mxu(one_hot((2 * channels, channels), lambda r, c: r // 2 == c), lift_ref[...])
    at_row = iota(lift_rows.shape, 0) % 2
    lift_pair = jnp.concatenate([jnp.where(at_row == half, lift_rows, 0.0) for half in range(2)], axis=1)
    lift_pair = lift_pair.astype(BF16)
    head_rows = mxu(one_hot((PAIR * channels, channels), lambda r, c: r // PAIR == c), head_ref[...])
    at_row = iota(head_rows.shape, 0) % PAIR // POOL
    head_pair = jnp.concatenate([jnp.where(at_row == half, head_rows, 0.0) for half in range(2)], axis=1)
    head_pair = head_pair.astype(BF16)
    stage_ref[:, :, :8] = jnp.zeros(stage_ref.shape[:2] + (8, width), F32)
    stage_ref[:, :, 8 + block_cols :] = jnp.zeros(stage_ref.shape[:2] + (8, width), F32)

    strip_rule = pool_of(2, channels)
    pair_rule = pool_of(1, channels)
    low_rows = 2 * channels

    def lows_of(cells):
        low = pooled(strip_rule, cells)
        return [low[:low_rows], low[low_rows:]]

    def lifted(low):
        act = mxu(mxu(pick, low.astype(BF16), NT).astype(BF16), lift_pair)
        return act.astype(BF16).astype(F32)

    own_low = lows_of(coarse_ref[...])
    own_act = [lifted(low) for low in own_low]
    finish(0)
    finish(1)
    above_low = lows_of(halo_ref[0])
    below_low = lows_of(halo_ref[1])
    acts = [lifted(low) for low in above_low] + own_act + [lifted(low) for low in below_low]
    domain_rows = count * block_rows
    layers = conv_ref.shape[0]
    cells = [[act[:, half * width : (half + 1) * width] for act in acts] for half in range(2)]
    for layer in range(layers):
        parts = shifts(cells, lambda half, at: stage_ref.at[half, at])
        act = residual_pairs(parts, taps_ref[layer], block_cols).astype(F32)
        cells = []
        for half in range(2):
            runs = []
            for pair in range(act.shape[0] // block_cols):
                run = act[pair * block_cols : (pair + 1) * block_cols, half * width : (half + 1) * width]
                row = 2 * pair + half + layer + 1 - block_rows
                if not 0 <= row < block_rows:
                    place = mine * block_rows + row
                    run = jnp.where(jnp.logical_and(place >= 0, place < domain_rows), run, 0.0)
                runs.append(run)
            cells.append(runs)

    above = halo_ref[0].astype(F32)
    own = coarse_ref[...].astype(F32)
    below = halo_ref[1].astype(F32)
    fields = [above[:, PAIR:], own[:, :PAIR], own[:, PAIR:], below[:, :PAIR]]
    lows = [above_low[1]] + own_low + [below_low[0]]
    for pair in range(4):
        act = jnp.concatenate([cells[half][pair] for half in range(2)], axis=1).astype(BF16)
        rest = mxu(head_pair, act, NT)
        wide = 0.0
        for _ in range(3):
            part = rest.astype(BF16)
            wide = wide + mxu(part, spread)
            rest = rest - part.astype(F32)
        mean = fields[pair] + wide.reshape(channels, PAIR, col_total)
        if 1 <= pair <= 2:
            mean_ref[:, (pair - 1) * PAIR : pair * PAIR] = mean
        low = pooled(pair_rule, mean.reshape(PAIR * channels, col_total).astype(BF16))
        clow_ref[pair] = jnp.concatenate([low, lows[pair]], axis=0).astype(BF16)
    for index in range(2, len(moves)):
        finish(index)


def edge(coarse, noise, table, lift, conv, head, span):
    channels, strip_rows, col_total = coarse.shape
    layers, _, width, _ = conv.shape
    vmem = pl.BlockSpec(memory_space=pltpu.VMEM)
    copies = span + 3
    return pl.pallas_call(
        functools.partial(edge_kernel, span),
        out_shape=(
            jax.ShapeDtypeStruct((4, 4 * channels, col_total), BF16),
            jax.ShapeDtypeStruct((4, 4 * channels, col_total), BF16),
            jax.ShapeDtypeStruct(coarse.shape, F32),
            jax.ShapeDtypeStruct((span, 1, 128), jnp.int32),
        ),
        in_specs=[vmem] * 6,
        out_specs=(vmem,) * 4,
        scratch_shapes=[
            pltpu.VMEM((2,) + coarse.shape, BF16),
            pltpu.VMEM((layers, 12 * width, 2 * width), BF16),
            pltpu.VMEM((2, 3 * strip_rows // PAIR, col_total // POOL + 16, width), F32),
            pltpu.SemaphoreType.DMA((copies,)),
            pltpu.SemaphoreType.DMA((copies,)),
        ],
        compiler_params=pltpu.CompilerParams(collective_id=0, has_side_effects=True),
        name="edge",
    )(coarse, noise, table, lift, conv, head)


def patch_kernel(
    slot_total,
    table_ref,
    nlow_ref,
    clow_ref,
    mean_ref,
    noise_ref,
    weight_ref,
    lift_ref,
    conv_ref,
    head_ref,
    out_mean_ref,
    out_var_ref,
    taps_ref,
    field_ref,
    wide_ref,
    acc_ref,
    den_ref,
    stage_ref,
    list_ref,
):
    feat_rows, strip_rows, col_total = noise_ref.shape
    channels = mean_ref.shape[0]
    members = feat_rows // channels
    width = lift_ref.shape[1]
    patch = weight_ref.shape[0]
    span = patch // strip_rows
    block_cols = patch // POOL
    offsets = col_total // POOL
    pad = 8

    build_taps(conv_ref, taps_ref)
    acc_ref[...] = jnp.zeros_like(acc_ref)
    den_ref[...] = jnp.zeros_like(den_ref)
    wide_ref[...] = jnp.zeros_like(wide_ref)
    wide_ref[:, :patch] = weight_ref[...].astype(F32)

    low_rows = 2 * feat_rows + 4 * channels
    noise_rows = 2 * feat_rows

    def source(row, column):
        noise_at = (row // 2) % channels
        cond_at = channels + (row - noise_rows) // 2
        return column == jnp.where(row < noise_rows, noise_at, cond_at)

    base = mxu(one_hot((low_rows, 3 * channels), source), lift_ref[...])
    row = iota(base.shape, 0)
    blocks = []
    for member in range(members):
        first = 2 * channels * member
        for half in range(2):
            keep = (row >= first) & (row < first + 2 * channels) & (row % 2 == half)
            blocks.append(jnp.where(keep, base, 0.0))
    noise_lift = jnp.concatenate(blocks, axis=1).astype(BF16)
    cond_lift = jnp.concatenate(
        [jnp.where((row >= noise_rows) & (row % 2 == half), base, 0.0) for half in range(2)], axis=1
    ).astype(BF16)
    order = one_hot((col_total, col_total), lambda r, c: c == POOL * (r % offsets) + r // offsets)
    for pair in range(4):
        low = jnp.concatenate([nlow_ref[pair], clow_ref[pair]], axis=0)
        turned = mxu(order, low, NT).astype(BF16)
        cond = mxu(turned, cond_lift)
        act = in_gain * mxu(turned, noise_lift) + jnp.concatenate([cond] * members, axis=1)
        act = act.astype(BF16).astype(F32)
        for phase in range(POOL):
            for member in range(members):
                for half in range(2):
                    first = (member * 2 + half) * width
                    field_ref[phase, pair * members + member, half, pad : pad + offsets] = act[
                        phase * offsets : (phase + 1) * offsets, first : first + width
                    ]

    lanes = 128
    head_wide = one_hot((channels, lanes), lambda r, c: (c % channels == r) & (c < 4 * feat_rows))
    head_wide = mxu(head_ref[...], head_wide, TN)
    lane = iota(head_wide.shape, 1)
    heads = []
    for pair in range(2):
        for member in range(members):
            for half in range(2):
                first = (2 * pair + half) * feat_rows + member * channels
                keep = (lane >= first) & (lane < first + channels)
                heads.append(jnp.where(keep, head_wide, 0.0))
    heads = jnp.concatenate(heads, axis=0).astype(BF16)

    group = GROUP
    slots = 4 * members
    stage_ref[...] = jnp.zeros_like(stage_ref)
    field_ref[:, slots] = jnp.zeros(field_ref.shape[:1] + field_ref.shape[2:], F32)
    stride = group * members * block_cols
    reach = 3 * lanes

    def note(index, found):
        offset = index // slot_total
        slot = index - offset * slot_total
        live = slot < table_ref[offset, 0, slot_total]

        @pl.when(live)
        def _():
            list_ref[found] = index

        return found + live.astype(jnp.int32)

    def blank(index, carry):
        list_ref[index] = 0
        return carry

    lax.fori_loop(0, list_ref.shape[0], blank, 0)
    live_total = lax.fori_loop(0, span * slot_total, note, 0)

    def step(turn, carry):
        pieces = []
        for at in range(group):
            place = turn * group + at
            index = list_ref[place]
            offset = index // slot_total
            column = table_ref[offset, 0, index - offset * slot_total]
            pieces.append((offset, column, place < live_total))
        edge_cell = iota((8, width), 0)
        parts = []
        for tap in range(3):
            sides = []
            for half in range(2):
                rows = []
                for pair in range(4):
                    for offset, column, _ in pieces:
                        phase = column & (POOL - 1)
                        window = pl.ds((column >> 2) + pad + tap - 1, block_cols)
                        for member in range(members):
                            which = pair * members + member
                            if pair == 0:
                                which = jnp.where(offset == 0, slots, which)
                            if pair == 3:
                                which = jnp.where(offset == span - 1, slots, which)
                            at = field_ref[phase, which, half, window, :]
                            if tap == 0:
                                at = jnp.concatenate([jnp.where(edge_cell == 0, 0.0, at[:8]), at[8:]], axis=0)
                            if tap == 2:
                                at = jnp.concatenate([at[:-8], jnp.where(edge_cell == 7, 0.0, at[-8:])], axis=0)
                            rows.append(at)
                sides.append(jnp.concatenate(rows, axis=0))
            parts.append(jnp.concatenate(sides, axis=1).astype(BF16))
        act = residual_pairs(parts, taps_ref[0], stride).astype(F32)
        cells = []
        for half in range(2):
            runs = []
            for pair in range(3):
                for at, (offset, _, _) in enumerate(pieces):
                    for member in range(members):
                        first = len(runs) * block_cols
                        run = act[first : first + block_cols, half * width : (half + 1) * width]
                        if pair == 0 and half == 0:
                            run = jnp.where(offset == 0, 0.0, run)
                        if pair == 2 and half == 1:
                            run = jnp.where(offset == span - 1, 0.0, run)
                        runs.append(run)
            cells.append(runs)
        parts = shifts(cells, lambda half, at: stage_ref.at[half, at])
        act = residual_pairs(parts, taps_ref[1], stride).astype(F32)
        rows = []
        for at in range(group):
            sides = []
            for pair in range(2):
                for member in range(members):
                    first = ((pair * group + at) * members + member) * block_cols
                    sides.append(act[first : first + block_cols])
            rows.append(jnp.concatenate(sides, axis=1))
        terms = mxu(jnp.concatenate(rows, axis=0).astype(BF16), heads)
        cols = iota((block_cols, reach), 1)
        blocks = iota((block_cols, reach), 0)
        for at, (offset, column, live) in enumerate(pieces):
            term = terms[at * block_cols : (at + 1) * block_cols]
            high = term.astype(BF16)
            low = (term - high.astype(F32)).astype(BF16)
            first = jnp.minimum(column // lanes, col_total // lanes - 3) * lanes
            inner = column - first
            span_cols = pl.ds(pl.multiple_of(first, lanes), reach)
            place = jnp.where(((cols - inner) >> 2) == blocks, 1.0, 0.0).astype(BF16)
            placed = mxu(high, place, TN) + mxu(low, place, TN)
            top = pl.multiple_of(offset * strip_rows, strip_rows)
            weights = pltpu.roll(wide_ref[pl.ds(top, strip_rows), :], inner, axis=1)
            weights = jnp.where(live, weights, 0.0)
            den_ref[:, span_cols] += weights
            for row in range(strip_rows):
                below = (row // POOL) * feat_rows
                acc_ref[row, :, span_cols] += weights[row : row + 1, :] * placed[below : below + feat_rows, :]
        return carry

    lax.fori_loop(0, (live_total + group - 1) // group, step, 0)

    denom = den_ref[...]
    scale = 1.0 / jnp.maximum(denom, 1.0)
    for channel in range(channels):
        outs = []
        for member in range(members):
            at = member * channels + channel
            numer = skip_gain * noise_ref[at].astype(F32) * denom + out_gain * acc_ref[:, at, :]
            outs.append(mean_ref[channel] + numer * scale)
        ens_mean = sum(outs) * (1.0 / members)
        out_mean_ref[channel] = ens_mean
        out_var_ref[channel] = sum((out - ens_mean) ** 2 for out in outs) * (1.0 / members)


def patches(tables, nlow, clow, mean, noise, weights, lift, conv, head, slot_total):
    feat_rows, strip_rows, col_total = noise.shape
    layers, _, width, _ = conv.shape
    members = feat_rows // mean.shape[0]
    vmem = pl.BlockSpec(memory_space=pltpu.VMEM)
    return pl.pallas_call(
        functools.partial(patch_kernel, slot_total),
        out_shape=(jax.ShapeDtypeStruct(mean.shape, F32),) * 2,
        in_specs=[pl.BlockSpec(memory_space=pltpu.SMEM)] + [vmem] * 8,
        out_specs=(vmem, vmem),
        scratch_shapes=[
            pltpu.VMEM((layers, 12 * width, 2 * width), BF16),
            pltpu.VMEM((POOL, 4 * members + 1, 2, col_total // POOL + 16, width), F32),
            pltpu.VMEM((weights.shape[0], 3 * 128), F32),
            pltpu.VMEM((strip_rows, feat_rows, col_total), F32),
            pltpu.VMEM((strip_rows, col_total), F32),
            pltpu.VMEM((2, GROUP * 3 * members, weights.shape[0] // POOL + 16, width), F32),
            pltpu.SMEM((weights.shape[0] // strip_rows * slot_total + GROUP,), jnp.int32),
        ],
        name="patches",
    )(tables, nlow, clow, mean, noise, weights, lift, conv, head)


def local(
    coarse,
    noise_field,
    anchors,
    counts,
    blend_weights,
    regress_lift,
    regress_conv,
    regress_head,
    denoise_lift,
    denoise_conv,
    denoise_head,
):
    members, channels, strip_rows, col_total = noise_field.shape
    span = blend_weights.shape[0] // strip_rows
    slot_total = anchors.shape[1]
    noise = noise_field.reshape(members * channels, strip_rows, col_total)
    table = jnp.concatenate([anchors, counts[:, None]], axis=1)
    table = jnp.pad(table, ((0, 0), (0, 127 - slot_total)))[None]
    nlow, clow, mean, tables = edge(coarse, noise, table, regress_lift, regress_conv, regress_head.T, span)
    return patches(
        tables, nlow, clow, mean, noise, blend_weights, denoise_lift, denoise_conv, denoise_head.T, slot_total
    )


def solution(mesh):
    in_specs = (
        P(None, ("groups", "tile"), None),
        P(None, None, ("groups", "tile"), None),
        P(("groups", "tile"), None),
        P(("groups", "tile")),
        P(),
        P(),
        P(),
        P(),
        P(),
        P(),
        P(),
    )
    out_specs = (P(None, ("groups", "tile"), None), P(None, ("groups", "tile"), None))
    return jax.shard_map(local, mesh=mesh, in_specs=in_specs, out_specs=out_specs, check_vma=False)
```

```python
import functools
import math

import jax
import jax.numpy as jnp
from jax import lax
from jax.experimental import pallas as pl
from jax.experimental.pallas import tpu as pltpu
from jax.sharding import PartitionSpec as P

POOL = 4
PAIR = 2 * POOL
GROUP = 3

skip_gain = 0.2
out_gain = 0.5 / math.sqrt(1.25)
in_gain = 1.0 / math.sqrt(1.25)

BF16 = jnp.bfloat16
F32 = jnp.float32
NN = (((1,), (0,)), ((), ()))
NT = (((1,), (1,)), ((), ()))
TN = (((0,), (0,)), ((), ()))


def mxu(lhs, rhs, dims=NN):
    return lax.dot_general(lhs, rhs, dims, preferred_element_type=F32)


def iota(shape, axis):
    return lax.broadcasted_iota(jnp.int32, shape, axis)


def one_hot(shape, rule):
    return jnp.where(rule(iota(shape, 0), iota(shape, 1)), 1.0, 0.0).astype(BF16)


def pool_of(pairs, channels):
    depth = PAIR * pairs

    def rule(row, column):
        pair = row // (2 * channels)
        channel = row % (2 * channels) // 2
        block = 2 * pair + row % 2
        return (channel == column // depth) & (block == column % depth // POOL)

    return one_hot((2 * pairs * channels, depth * channels), rule)


def pooled(rule, cells):
    cols = cells.shape[-1]
    sums = mxu(rule, cells.reshape(-1, cols))
    sums = sums + pltpu.roll(sums, cols - 1, 1)
    sums = sums + pltpu.roll(sums, cols - 2, 1)
    return sums * (1.0 / (POOL * POOL))


def build_taps(conv_ref, taps_ref):
    width = conv_ref.shape[2]
    for layer in range(conv_ref.shape[0]):
        for tap in range(3):
            for row_in in range(4):
                for row_out in range(2):
                    at = row_in - row_out
                    rows = pl.ds((tap * 4 + row_in) * width, width)
                    block = jnp.zeros((width, width), BF16)
                    if 0 <= at < 3:
                        block = conv_ref[layer, 3 * at + tap]
                    if tap * 4 + row_in >= 6:
                        block = -block
                    taps_ref[layer, rows, row_out * width : (row_out + 1) * width] = block


def shifts(cells, holds):
    parts = [[], [], []]
    for half, runs in enumerate(cells):
        rows = [[], [], []]
        for at, run in enumerate(runs):
            count = run.shape[0]
            hold = holds(half, at)
            hold[8 : 8 + count] = run
            rows[0].append(hold[7 : 7 + count])
            rows[1].append(run)
            rows[2].append(hold[9 : 9 + count])
        for tap in range(3):
            parts[tap].append(jnp.concatenate(rows[tap], axis=0))
    return [jnp.concatenate(sides, axis=1).astype(BF16) for sides in parts]


def residual_pairs(parts, taps, stride):
    total, lanes = parts[0].shape
    count = total - stride
    half = lanes // 2
    pieces = [piece for part in parts for piece in (part[:count], part[stride:])]
    depth = taps.shape[0] // 2
    term = mxu(jnp.concatenate(pieces[:3], axis=1), taps[:depth])
    term = term - mxu(jnp.concatenate(pieces[3:], axis=1), taps[depth:])
    center = jnp.concatenate([parts[1][:count, half:], parts[1][stride:, :half]], axis=1)
    term = center.astype(F32) + term * jax.nn.sigmoid(term)
    return term.astype(BF16)


def edge_kernel(
    span,
    coarse_ref,
    noise_ref,
    table_ref,
    lift_ref,
    conv_ref,
    head_ref,
    nlow_ref,
    clow_ref,
    mean_ref,
    tables_ref,
    rows_ref,
    halo_ref,
    own_ref,
    far_ref,
    taps_ref,
    stage_ref,
    send_sem,
    recv_sem,
):
    channels, strip_rows, col_total = coarse_ref.shape
    width = lift_ref.shape[1]
    block_cols = col_total // POOL
    block_rows = strip_rows // POOL
    mine = lax.axis_index("tile")
    count = lax.axis_size("tile")
    barrier = pltpu.get_barrier_semaphore()

    def holds(place):
        return jnp.logical_and(place >= 0, place < count)

    moves = [
        (rows_ref.at[1], halo_ref.at[0], 1),
        (rows_ref.at[0], halo_ref.at[1], -1),
        (own_ref.at[0], far_ref.at[0], 1),
        (own_ref.at[1], far_ref.at[1], -1),
        (nlow_ref.at[2], nlow_ref.at[0], 1),
        (nlow_ref.at[1], nlow_ref.at[3], -1),
    ]
    moves = moves + [(table_ref.at[0], tables_ref.at[at], at) for at in range(span - 1, 0, -1)]
    steps = sorted({move[2] for move in moves})
    for step in steps:
        pl.semaphore_signal(
            barrier,
            inc=1,
            device_id={"tile": lax.rem(mine - step + count, count)},
            device_id_type=pl.DeviceIdType.MESH,
        )

    def copy_of(index):
        source, target, step = moves[index]
        return pltpu.make_async_remote_copy(
            src_ref=source,
            dst_ref=target,
            send_sem=send_sem.at[index],
            recv_sem=recv_sem.at[index],
            device_id={"tile": mine + step},
            device_id_type=pl.DeviceIdType.MESH,
        )

    def start(index):
        @pl.when(holds(mine + moves[index][2]))
        def _():
            copy_of(index).start()

    def arrive(index):
        @pl.when(holds(mine - moves[index][2]))
        def _():
            copy_of(index).wait_recv()

    def leave(index):
        @pl.when(holds(mine + moves[index][2]))
        def _():
            copy_of(index).wait_send()

    def clear(index):
        target, step = moves[index][1:]

        @pl.when(jnp.logical_not(holds(mine - step)))
        def _():
            target[...] = jnp.zeros(target.shape, target.dtype)

    low = pooled(pool_of(2, 2 * channels), noise_ref[...]).astype(BF16)
    for pair in range(2):
        nlow_ref[1 + pair] = low[pair * 4 * channels : (pair + 1) * 4 * channels]
    pick = one_hot((block_cols, col_total), lambda r, c: c == POOL * r)
    spread = one_hot((block_cols, col_total), lambda r, c: c // POOL == r)
    lift_rows = mxu(one_hot((2 * channels, channels), lambda r, c: r // 2 == c), lift_ref[...])
    at_row = iota(lift_rows.shape, 0) % 2
    lift_pair = jnp.concatenate([jnp.where(at_row == half, lift_rows, 0.0) for half in range(2)], axis=1)
    lift_pair = lift_pair.astype(BF16)
    head_rows = mxu(one_hot((PAIR * channels, channels), lambda r, c: r // PAIR == c), head_ref[...])
    at_row = iota(head_rows.shape, 0) % PAIR // POOL
    head_pair = jnp.concatenate([jnp.where(at_row == half, head_rows, 0.0) for half in range(2)], axis=1)
    head_pair = head_pair.astype(BF16)
    stage_ref[:, :, :8] = jnp.zeros(stage_ref.shape[:2] + (8, width), F32)
    stage_ref[:, :, 8 + block_cols :] = jnp.zeros(stage_ref.shape[:2] + (8, width), F32)

    strip_rule = pool_of(2, channels)
    pair_rule = pool_of(1, channels)
    low_rows = 2 * channels

    def lifted(low):
        act = mxu(mxu(pick, low, NT).astype(BF16), lift_pair)
        return act.astype(BF16).astype(F32)

    own = coarse_ref[...].astype(F32)
    own = [own[:, :PAIR], own[:, PAIR:]]
    low = pooled(strip_rule, coarse_ref[...]).astype(BF16)
    own_low = [low[:low_rows], low[low_rows:]]
    for pair in range(2):
        rows_ref[pair] = own[pair].reshape(PAIR * channels, col_total).astype(BF16)
        own_ref[pair] = own_low[pair]
    build_taps(conv_ref, taps_ref)
    own_act = [lifted(low) for low in own_low]
    for index in range(len(moves)):
        clear(index)
    tables_ref[0] = table_ref[0]
    pl.semaphore_wait(barrier, len(steps))
    for index in list(range(6, len(moves))) + list(range(6)):
        start(index)
    for index in range(4):
        arrive(index)
    near = [pooled(pair_rule, halo_ref[at]).astype(BF16) for at in range(2)]
    acts = [lifted(far_ref[0]), lifted(near[0])] + own_act + [lifted(near[1]), lifted(far_ref[1])]
    domain_rows = count * block_rows
    layers = conv_ref.shape[0]
    cells = [[act[:, half * width : (half + 1) * width] for act in acts] for half in range(2)]
    for layer in range(layers):
        parts = shifts(cells, lambda half, at: stage_ref.at[half, at])
        act = residual_pairs(parts, taps_ref[layer], block_cols).astype(F32)
        cells = []
        for half in range(2):
            runs = []
            for pair in range(act.shape[0] // block_cols):
                run = act[pair * block_cols : (pair + 1) * block_cols, half * width : (half + 1) * width]
                row = 2 * pair + half + layer + 1 - block_rows
                if not 0 <= row < block_rows:
                    place = mine * block_rows + row
                    run = jnp.where(jnp.logical_and(place >= 0, place < domain_rows), run, 0.0)
                runs.append(run)
            cells.append(runs)

    above, below = [halo_ref[at].astype(F32).reshape(own[0].shape) for at in range(2)]
    fields = [above] + own + [below]
    lows = near[:1] + own_low + near[1:]
    for pair in range(4):
        act = jnp.concatenate([cells[half][pair] for half in range(2)], axis=1).astype(BF16)
        rest = mxu(head_pair, act, NT)
        wide = 0.0
        for _ in range(3):
            part = rest.astype(BF16)
            wide = wide + mxu(part, spread)
            rest = rest - part.astype(F32)
        mean = fields[pair] + wide.reshape(channels, PAIR, col_total)
        if 1 <= pair <= 2:
            mean_ref[:, (pair - 1) * PAIR : pair * PAIR] = mean
        low = pooled(pair_rule, mean.reshape(PAIR * channels, col_total).astype(BF16))
        clow_ref[pair] = jnp.concatenate([low, lows[pair].astype(F32)], axis=0).astype(BF16)
    for index in range(4, len(moves)):
        arrive(index)
    for index in range(len(moves)):
        leave(index)


def edge(coarse, noise, table, lift, conv, head, span):
    channels, strip_rows, col_total = coarse.shape
    layers, _, width, _ = conv.shape
    vmem = pl.BlockSpec(memory_space=pltpu.VMEM)
    copies = span + 5
    return pl.pallas_call(
        functools.partial(edge_kernel, span),
        out_shape=(
            jax.ShapeDtypeStruct((4, 4 * channels, col_total), BF16),
            jax.ShapeDtypeStruct((4, 4 * channels, col_total), BF16),
            jax.ShapeDtypeStruct(coarse.shape, F32),
            jax.ShapeDtypeStruct((span, 1, 128), jnp.int32),
        ),
        in_specs=[vmem] * 6,
        out_specs=(vmem,) * 4,
        scratch_shapes=[
            pltpu.VMEM((2, PAIR * channels, col_total), BF16),
            pltpu.VMEM((2, PAIR * channels, col_total), BF16),
            pltpu.VMEM((2, 2 * channels, col_total), BF16),
            pltpu.VMEM((2, 2 * channels, col_total), BF16),
            pltpu.VMEM((layers, 12 * width, 2 * width), BF16),
            pltpu.VMEM((2, 3 * strip_rows // PAIR, col_total // POOL + 16, width), F32),
            pltpu.SemaphoreType.DMA((copies,)),
            pltpu.SemaphoreType.DMA((copies,)),
        ],
        compiler_params=pltpu.CompilerParams(collective_id=0, has_side_effects=True),
        name="edge",
    )(coarse, noise, table, lift, conv, head)


def patch_kernel(
    slot_total,
    table_ref,
    nlow_ref,
    clow_ref,
    mean_ref,
    noise_ref,
    weight_ref,
    lift_ref,
    conv_ref,
    head_ref,
    out_mean_ref,
    out_var_ref,
    taps_ref,
    field_ref,
    wide_ref,
    acc_ref,
    den_ref,
    stage_ref,
    list_ref,
):
    feat_rows, strip_rows, col_total = noise_ref.shape
    channels = mean_ref.shape[0]
    members = feat_rows // channels
    width = lift_ref.shape[1]
    patch = weight_ref.shape[0]
    span = patch // strip_rows
    block_cols = patch // POOL
    offsets = col_total // POOL
    pad = 8

    build_taps(conv_ref, taps_ref)
    acc_ref[...] = jnp.zeros_like(acc_ref)
    den_ref[...] = jnp.zeros_like(den_ref)
    wide_ref[...] = jnp.zeros_like(wide_ref)
    wide_ref[:, :patch] = weight_ref[...].astype(F32)

    low_rows = 2 * feat_rows + 4 * channels
    noise_rows = 2 * feat_rows

    def source(row, column):
        noise_at = (row // 2) % channels
        cond_at = channels + (row - noise_rows) // 2
        return column == jnp.where(row < noise_rows, noise_at, cond_at)

    base = mxu(one_hot((low_rows, 3 * channels), source), lift_ref[...])
    row = iota(base.shape, 0)
    blocks = []
    for member in range(members):
        first = 2 * channels * member
        for half in range(2):
            keep = (row >= first) & (row < first + 2 * channels) & (row % 2 == half)
            blocks.append(jnp.where(keep, base, 0.0))
    noise_lift = jnp.concatenate(blocks, axis=1).astype(BF16)
    cond_lift = jnp.concatenate(
        [jnp.where((row >= noise_rows) & (row % 2 == half), base, 0.0) for half in range(2)], axis=1
    ).astype(BF16)
    order = one_hot((col_total, col_total), lambda r, c: c == POOL * (r % offsets) + r // offsets)
    for pair in range(4):
        low = jnp.concatenate([nlow_ref[pair], clow_ref[pair]], axis=0)
        turned = mxu(order, low, NT).astype(BF16)
        cond = mxu(turned, cond_lift)
        act = in_gain * mxu(turned, noise_lift) + jnp.concatenate([cond] * members, axis=1)
        act = act.astype(BF16).astype(F32)
        for phase in range(POOL):
            for member in range(members):
                for half in range(2):
                    first = (member * 2 + half) * width
                    field_ref[phase, pair * members + member, half, pad : pad + offsets] = act[
                        phase * offsets : (phase + 1) * offsets, first : first + width
                    ]

    lanes = 128
    head_wide = one_hot((channels, lanes), lambda r, c: (c % channels == r) & (c < 4 * feat_rows))
    head_wide = mxu(head_ref[...], head_wide, TN)
    lane = iota(head_wide.shape, 1)
    heads = []
    for pair in range(2):
        for member in range(members):
            for half in range(2):
                first = (2 * pair + half) * feat_rows + member * channels
                keep = (lane >= first) & (lane < first + channels)
                heads.append(jnp.where(keep, head_wide, 0.0))
    heads = jnp.concatenate(heads, axis=0).astype(BF16)

    group = GROUP
    slots = 4 * members
    stage_ref[...] = jnp.zeros_like(stage_ref)
    field_ref[:, slots] = jnp.zeros(field_ref.shape[:1] + field_ref.shape[2:], F32)
    stride = group * members * block_cols
    reach = 3 * lanes

    def note(index, found):
        offset = index // slot_total
        slot = index - offset * slot_total
        live = slot < table_ref[offset, 0, slot_total]

        @pl.when(live)
        def _():
            list_ref[found] = index

        return found + live.astype(jnp.int32)

    def blank(index, carry):
        list_ref[index] = 0
        return carry

    lax.fori_loop(0, list_ref.shape[0], blank, 0)
    live_total = lax.fori_loop(0, span * slot_total, note, 0)

    def step(turn, carry):
        pieces = []
        for at in range(group):
            place = turn * group + at
            index = list_ref[place]
            offset = index // slot_total
            column = table_ref[offset, 0, index - offset * slot_total]
            pieces.append((offset, column, place < live_total))
        edge_cell = iota((8, width), 0)
        parts = []
        for tap in range(3):
            sides = []
            for half in range(2):
                rows = []
                for pair in range(4):
                    for offset, column, _ in pieces:
                        phase = column & (POOL - 1)
                        window = pl.ds((column >> 2) + pad + tap - 1, block_cols)
                        for member in range(members):
                            which = pair * members + member
                            if pair == 0:
                                which = jnp.where(offset == 0, slots, which)
                            if pair == 3:
                                which = jnp.where(offset == span - 1, slots, which)
                            at = field_ref[phase, which, half, window, :]
                            if tap == 0:
                                at = jnp.concatenate([jnp.where(edge_cell == 0, 0.0, at[:8]), at[8:]], axis=0)
                            if tap == 2:
                                at = jnp.concatenate([at[:-8], jnp.where(edge_cell == 7, 0.0, at[-8:])], axis=0)
                            rows.append(at)
                sides.append(jnp.concatenate(rows, axis=0))
            parts.append(jnp.concatenate(sides, axis=1).astype(BF16))
        act = residual_pairs(parts, taps_ref[0], stride).astype(F32)
        cells = []
        for half in range(2):
            runs = []
            for pair in range(3):
                for at, (offset, _, _) in enumerate(pieces):
                    for member in range(members):
                        first = len(runs) * block_cols
                        run = act[first : first + block_cols, half * width : (half + 1) * width]
                        if pair == 0 and half == 0:
                            run = jnp.where(offset == 0, 0.0, run)
                        if pair == 2 and half == 1:
                            run = jnp.where(offset == span - 1, 0.0, run)
                        runs.append(run)
            cells.append(runs)
        parts = shifts(cells, lambda half, at: stage_ref.at[half, at])
        act = residual_pairs(parts, taps_ref[1], stride).astype(F32)
        rows = []
        for at in range(group):
            sides = []
            for pair in range(2):
                for member in range(members):
                    first = ((pair * group + at) * members + member) * block_cols
                    sides.append(act[first : first + block_cols])
            rows.append(jnp.concatenate(sides, axis=1))
        terms = mxu(jnp.concatenate(rows, axis=0).astype(BF16), heads)
        cols = iota((block_cols, reach), 1)
        blocks = iota((block_cols, reach), 0)
        for at, (offset, column, live) in enumerate(pieces):
            term = terms[at * block_cols : (at + 1) * block_cols]
            high = term.astype(BF16)
            low = (term - high.astype(F32)).astype(BF16)
            first = jnp.minimum(column // lanes, col_total // lanes - 3) * lanes
            inner = column - first
            span_cols = pl.ds(pl.multiple_of(first, lanes), reach)
            place = jnp.where(((cols - inner) >> 2) == blocks, 1.0, 0.0).astype(BF16)
            placed = mxu(high, place, TN) + mxu(low, place, TN)
            top = pl.multiple_of(offset * strip_rows, strip_rows)
            weights = pltpu.roll(wide_ref[pl.ds(top, strip_rows), :], inner, axis=1)
            weights = jnp.where(live, weights, 0.0)
            den_ref[:, span_cols] += weights
            for row in range(strip_rows):
                below = (row // POOL) * feat_rows
                acc_ref[row, :, span_cols] += weights[row : row + 1, :] * placed[below : below + feat_rows, :]
        return carry

    lax.fori_loop(0, (live_total + group - 1) // group, step, 0)

    denom = den_ref[...]
    scale = 1.0 / jnp.maximum(denom, 1.0)
    for channel in range(channels):
        outs = []
        for member in range(members):
            at = member * channels + channel
            numer = skip_gain * noise_ref[at].astype(F32) * denom + out_gain * acc_ref[:, at, :]
            outs.append(mean_ref[channel] + numer * scale)
        ens_mean = sum(outs) * (1.0 / members)
        out_mean_ref[channel] = ens_mean
        out_var_ref[channel] = sum((out - ens_mean) ** 2 for out in outs) * (1.0 / members)


def patches(tables, nlow, clow, mean, noise, weights, lift, conv, head, slot_total):
    feat_rows, strip_rows, col_total = noise.shape
    layers, _, width, _ = conv.shape
    members = feat_rows // mean.shape[0]
    vmem = pl.BlockSpec(memory_space=pltpu.VMEM)
    return pl.pallas_call(
        functools.partial(patch_kernel, slot_total),
        out_shape=(jax.ShapeDtypeStruct(mean.shape, F32),) * 2,
        in_specs=[pl.BlockSpec(memory_space=pltpu.SMEM)] + [vmem] * 8,
        out_specs=(vmem, vmem),
        scratch_shapes=[
            pltpu.VMEM((layers, 12 * width, 2 * width), BF16),
            pltpu.VMEM((POOL, 4 * members + 1, 2, col_total // POOL + 16, width), F32),
            pltpu.VMEM((weights.shape[0], 3 * 128), F32),
            pltpu.VMEM((strip_rows, feat_rows, col_total), F32),
            pltpu.VMEM((strip_rows, col_total), F32),
            pltpu.VMEM((2, GROUP * 3 * members, weights.shape[0] // POOL + 16, width), F32),
            pltpu.SMEM((weights.shape[0] // strip_rows * slot_total + GROUP,), jnp.int32),
        ],
        name="patches",
    )(tables, nlow, clow, mean, noise, weights, lift, conv, head)


def local(
    coarse,
    noise_field,
    anchors,
    counts,
    blend_weights,
    regress_lift,
    regress_conv,
    regress_head,
    denoise_lift,
    denoise_conv,
    denoise_head,
):
    members, channels, strip_rows, col_total = noise_field.shape
    span = blend_weights.shape[0] // strip_rows
    slot_total = anchors.shape[1]
    noise = noise_field.reshape(members * channels, strip_rows, col_total)
    table = jnp.concatenate([anchors, counts[:, None]], axis=1)
    table = jnp.pad(table, ((0, 0), (0, 127 - slot_total)))[None]
    nlow, clow, mean, tables = edge(coarse, noise, table, regress_lift, regress_conv, regress_head.T, span)
    return patches(
        tables, nlow, clow, mean, noise, blend_weights, denoise_lift, denoise_conv, denoise_head.T, slot_total
    )


def solution(mesh):
    in_specs = (
        P(None, ("groups", "tile"), None),
        P(None, None, ("groups", "tile"), None),
        P(("groups", "tile"), None),
        P(("groups", "tile")),
        P(),
        P(),
        P(),
        P(),
        P(),
        P(),
        P(),
    )
    out_specs = (P(None, ("groups", "tile"), None), P(None, ("groups", "tile"), None))
    return jax.shard_map(local, mesh=mesh, in_specs=in_specs, out_specs=out_specs, check_vma=False)
```

```python
import functools
import math

import jax
import jax.numpy as jnp
from jax import lax
from jax.experimental import pallas as pl
from jax.experimental.pallas import tpu as pltpu
from jax.sharding import PartitionSpec as P

POOL = 4
PAIR = 2 * POOL
GROUP = 3

skip_gain = 0.2
out_gain = 0.5 / math.sqrt(1.25)
in_gain = 1.0 / math.sqrt(1.25)

BF16 = jnp.bfloat16
F32 = jnp.float32
NN = (((1,), (0,)), ((), ()))
NT = (((1,), (1,)), ((), ()))
TN = (((0,), (0,)), ((), ()))


def mxu(lhs, rhs, dims=NN):
    return lax.dot_general(lhs, rhs, dims, preferred_element_type=F32)


def iota(shape, axis):
    return lax.broadcasted_iota(jnp.int32, shape, axis)


def one_hot(shape, rule):
    return jnp.where(rule(iota(shape, 0), iota(shape, 1)), 1.0, 0.0).astype(BF16)


def pool_of(pairs, channels):
    depth = PAIR * pairs

    def rule(row, column):
        pair = row // (2 * channels)
        channel = row % (2 * channels) // 2
        block = 2 * pair + row % 2
        return (channel == column // depth) & (block == column % depth // POOL)

    return one_hot((2 * pairs * channels, depth * channels), rule)


def pooled(rule, cells):
    cols = cells.shape[-1]
    sums = mxu(rule, cells.reshape(-1, cols))
    sums = sums + pltpu.roll(sums, cols - 1, 1)
    sums = sums + pltpu.roll(sums, cols - 2, 1)
    return sums * (1.0 / (POOL * POOL))


def build_taps(conv_ref, taps_ref):
    width = conv_ref.shape[2]
    for layer in range(conv_ref.shape[0]):
        for tap in range(3):
            for row_in in range(4):
                for row_out in range(2):
                    at = row_in - row_out
                    rows = pl.ds((tap * 4 + row_in) * width, width)
                    block = jnp.zeros((width, width), BF16)
                    if 0 <= at < 3:
                        block = conv_ref[layer, 3 * at + tap]
                    if tap * 4 + row_in >= 6:
                        block = -block
                    taps_ref[layer, rows, row_out * width : (row_out + 1) * width] = block


def shifts(cells, holds):
    parts = [[], [], []]
    for half, runs in enumerate(cells):
        rows = [[], [], []]
        for at, run in enumerate(runs):
            count = run.shape[0]
            hold = holds(half, at)
            hold[8 : 8 + count] = run
            rows[0].append(hold[7 : 7 + count])
            rows[1].append(run)
            rows[2].append(hold[9 : 9 + count])
        for tap in range(3):
            parts[tap].append(jnp.concatenate(rows[tap], axis=0))
    return [jnp.concatenate(sides, axis=1).astype(BF16) for sides in parts]


def residual_pairs(parts, taps, stride):
    total, lanes = parts[0].shape
    count = total - stride
    half = lanes // 2
    pieces = [piece for part in parts for piece in (part[:count], part[stride:])]
    depth = taps.shape[0] // 2
    term = mxu(jnp.concatenate(pieces[:3], axis=1), taps[:depth])
    term = term - mxu(jnp.concatenate(pieces[3:], axis=1), taps[depth:])
    center = jnp.concatenate([parts[1][:count, half:], parts[1][stride:, :half]], axis=1)
    term = center.astype(F32) + term * jax.nn.sigmoid(term)
    return term.astype(BF16)


def fetch(pairs, sems):
    copies = [pltpu.make_async_copy(source, target, sems.at[at]) for at, (source, target) in enumerate(pairs)]
    for copy in copies:
        copy.start()
    return copies


def edge_kernel(
    span,
    coarse_hbm,
    noise_hbm,
    table_ref,
    lift_ref,
    conv_hbm,
    head_ref,
    nlow_ref,
    clow_ref,
    mean_ref,
    tables_ref,
    rows_ref,
    halo_ref,
    own_ref,
    far_ref,
    taps_ref,
    stage_ref,
    coarse_ref,
    noise_ref,
    conv_ref,
    load_sem,
    send_sem,
    recv_sem,
):
    channels, strip_rows, col_total = coarse_ref.shape
    width = lift_ref.shape[1]
    block_cols = col_total // POOL
    block_rows = strip_rows // POOL
    mine = lax.axis_index("tile")
    count = lax.axis_size("tile")
    barrier = pltpu.get_barrier_semaphore()

    def holds(place):
        return jnp.logical_and(place >= 0, place < count)

    moves = [
        (rows_ref.at[1], halo_ref.at[0], 1),
        (rows_ref.at[0], halo_ref.at[1], -1),
        (own_ref.at[0], far_ref.at[0], 1),
        (own_ref.at[1], far_ref.at[1], -1),
        (nlow_ref.at[2], nlow_ref.at[0], 1),
        (nlow_ref.at[1], nlow_ref.at[3], -1),
    ]
    moves = moves + [(table_ref.at[0], tables_ref.at[at], at) for at in range(span - 1, 0, -1)]
    steps = sorted({move[2] for move in moves})
    for step in steps:
        pl.semaphore_signal(
            barrier,
            inc=1,
            device_id={"tile": lax.rem(mine - step + count, count)},
            device_id_type=pl.DeviceIdType.MESH,
        )

    def copy_of(index):
        source, target, step = moves[index]
        return pltpu.make_async_remote_copy(
            src_ref=source,
            dst_ref=target,
            send_sem=send_sem.at[index],
            recv_sem=recv_sem.at[index],
            device_id={"tile": mine + step},
            device_id_type=pl.DeviceIdType.MESH,
        )

    def start(index):
        @pl.when(holds(mine + moves[index][2]))
        def _():
            copy_of(index).start()

    def arrive(index):
        @pl.when(holds(mine - moves[index][2]))
        def _():
            copy_of(index).wait_recv()

    def leave(index):
        @pl.when(holds(mine + moves[index][2]))
        def _():
            copy_of(index).wait_send()

    def clear(index):
        target, step = moves[index][1:]

        @pl.when(jnp.logical_not(holds(mine - step)))
        def _():
            target[...] = jnp.zeros(target.shape, target.dtype)

    loads = fetch([(coarse_hbm, coarse_ref), (noise_hbm, noise_ref), (conv_hbm, conv_ref)], load_sem)
    loads[1].wait()
    low = pooled(pool_of(2, 2 * channels), noise_ref[...]).astype(BF16)
    for pair in range(2):
        nlow_ref[1 + pair] = low[pair * 4 * channels : (pair + 1) * 4 * channels]
    pick = one_hot((block_cols, col_total), lambda r, c: c == POOL * r)
    spread = one_hot((block_cols, col_total), lambda r, c: c // POOL == r)
    lift_rows = mxu(one_hot((2 * channels, channels), lambda r, c: r // 2 == c), lift_ref[...])
    at_row = iota(lift_rows.shape, 0) % 2
    lift_pair = jnp.concatenate([jnp.where(at_row == half, lift_rows, 0.0) for half in range(2)], axis=1)
    lift_pair = lift_pair.astype(BF16)
    head_rows = mxu(one_hot((PAIR * channels, channels), lambda r, c: r // PAIR == c), head_ref[...])
    at_row = iota(head_rows.shape, 0) % PAIR // POOL
    head_pair = jnp.concatenate([jnp.where(at_row == half, head_rows, 0.0) for half in range(2)], axis=1)
    head_pair = head_pair.astype(BF16)
    stage_ref[:, :, :8] = jnp.zeros(stage_ref.shape[:2] + (8, width), F32)
    stage_ref[:, :, 8 + block_cols :] = jnp.zeros(stage_ref.shape[:2] + (8, width), F32)

    strip_rule = pool_of(2, channels)
    pair_rule = pool_of(1, channels)
    low_rows = 2 * channels

    def lifted(low):
        act = mxu(mxu(pick, low, NT).astype(BF16), lift_pair)
        return act.astype(BF16).astype(F32)

    loads[0].wait()
    own = coarse_ref[...].astype(F32)
    own = [own[:, :PAIR], own[:, PAIR:]]
    low = pooled(strip_rule, coarse_ref[...]).astype(BF16)
    own_low = [low[:low_rows], low[low_rows:]]
    for pair in range(2):
        rows_ref[pair] = own[pair].reshape(PAIR * channels, col_total).astype(BF16)
        own_ref[pair] = own_low[pair]
    loads[2].wait()
    build_taps(conv_ref, taps_ref)
    own_act = [lifted(low) for low in own_low]
    for index in range(len(moves)):
        clear(index)
    tables_ref[0] = table_ref[0]
    pl.semaphore_wait(barrier, len(steps))
    for index in list(range(6, len(moves))) + list(range(6)):
        start(index)
    for index in range(4):
        arrive(index)
    near = [pooled(pair_rule, halo_ref[at]).astype(BF16) for at in range(2)]
    acts = [lifted(far_ref[0]), lifted(near[0])] + own_act + [lifted(near[1]), lifted(far_ref[1])]
    domain_rows = count * block_rows
    layers = conv_ref.shape[0]
    cells = [[act[:, half * width : (half + 1) * width] for act in acts] for half in range(2)]
    for layer in range(layers):
        parts = shifts(cells, lambda half, at: stage_ref.at[half, at])
        act = residual_pairs(parts, taps_ref[layer], block_cols).astype(F32)
        cells = []
        for half in range(2):
            runs = []
            for pair in range(act.shape[0] // block_cols):
                run = act[pair * block_cols : (pair + 1) * block_cols, half * width : (half + 1) * width]
                row = 2 * pair + half + layer + 1 - block_rows
                if not 0 <= row < block_rows:
                    place = mine * block_rows + row
                    run = jnp.where(jnp.logical_and(place >= 0, place < domain_rows), run, 0.0)
                runs.append(run)
            cells.append(runs)

    above, below = [halo_ref[at].astype(F32).reshape(own[0].shape) for at in range(2)]
    fields = [above] + own + [below]
    lows = near[:1] + own_low + near[1:]
    for pair in range(4):
        act = jnp.concatenate([cells[half][pair] for half in range(2)], axis=1).astype(BF16)
        rest = mxu(head_pair, act, NT)
        wide = 0.0
        for _ in range(3):
            part = rest.astype(BF16)
            wide = wide + mxu(part, spread)
            rest = rest - part.astype(F32)
        mean = fields[pair] + wide.reshape(channels, PAIR, col_total)
        if 1 <= pair <= 2:
            mean_ref[:, (pair - 1) * PAIR : pair * PAIR] = mean
        low = pooled(pair_rule, mean.reshape(PAIR * channels, col_total).astype(BF16))
        clow_ref[pair] = jnp.concatenate([low, lows[pair].astype(F32)], axis=0).astype(BF16)
    for index in range(4, len(moves)):
        arrive(index)
    for index in range(len(moves)):
        leave(index)


def edge(coarse, noise, table, lift, conv, head, span):
    channels, strip_rows, col_total = coarse.shape
    layers, _, width, _ = conv.shape
    vmem = pl.BlockSpec(memory_space=pltpu.VMEM)
    far = pl.BlockSpec(memory_space=pl.ANY)
    copies = span + 5
    return pl.pallas_call(
        functools.partial(edge_kernel, span),
        out_shape=(
            jax.ShapeDtypeStruct((4, 4 * channels, col_total), BF16),
            jax.ShapeDtypeStruct((4, 4 * channels, col_total), BF16),
            jax.ShapeDtypeStruct(coarse.shape, F32),
            jax.ShapeDtypeStruct((span, 1, 128), jnp.int32),
        ),
        in_specs=[far, far, vmem, vmem, far, vmem],
        out_specs=(vmem,) * 4,
        scratch_shapes=[
            pltpu.VMEM((2, PAIR * channels, col_total), BF16),
            pltpu.VMEM((2, PAIR * channels, col_total), BF16),
            pltpu.VMEM((2, 2 * channels, col_total), BF16),
            pltpu.VMEM((2, 2 * channels, col_total), BF16),
            pltpu.VMEM((layers, 12 * width, 2 * width), BF16),
            pltpu.VMEM((2, 3 * strip_rows // PAIR, col_total // POOL + 16, width), F32),
            pltpu.VMEM(coarse.shape, BF16),
            pltpu.VMEM(noise.shape, BF16),
            pltpu.VMEM(conv.shape, BF16),
            pltpu.SemaphoreType.DMA((3,)),
            pltpu.SemaphoreType.DMA((copies,)),
            pltpu.SemaphoreType.DMA((copies,)),
        ],
        compiler_params=pltpu.CompilerParams(collective_id=0, has_side_effects=True),
        name="edge",
    )(coarse, noise, table, lift, conv, head)


def patch_kernel(
    slot_total,
    table_ref,
    nlow_ref,
    clow_ref,
    mean_hbm,
    noise_hbm,
    weight_hbm,
    lift_ref,
    conv_hbm,
    head_ref,
    out_mean_ref,
    out_var_ref,
    taps_ref,
    field_ref,
    wide_ref,
    acc_ref,
    den_ref,
    stage_ref,
    mean_ref,
    noise_ref,
    weight_ref,
    conv_ref,
    load_sem,
    list_ref,
):
    feat_rows, strip_rows, col_total = noise_ref.shape
    channels = mean_ref.shape[0]
    members = feat_rows // channels
    width = lift_ref.shape[1]
    patch = weight_ref.shape[0]
    span = patch // strip_rows
    block_cols = patch // POOL
    offsets = col_total // POOL
    pad = 8

    loads = fetch(
        [(conv_hbm, conv_ref), (weight_hbm, weight_ref), (mean_hbm, mean_ref), (noise_hbm, noise_ref)], load_sem
    )
    acc_ref[...] = jnp.zeros_like(acc_ref)
    den_ref[...] = jnp.zeros_like(den_ref)
    wide_ref[...] = jnp.zeros_like(wide_ref)

    low_rows = 2 * feat_rows + 4 * channels
    noise_rows = 2 * feat_rows

    def source(row, column):
        noise_at = (row // 2) % channels
        cond_at = channels + (row - noise_rows) // 2
        return column == jnp.where(row < noise_rows, noise_at, cond_at)

    base = mxu(one_hot((low_rows, 3 * channels), source), lift_ref[...])
    row = iota(base.shape, 0)
    blocks = []
    for member in range(members):
        first = 2 * channels * member
        for half in range(2):
            keep = (row >= first) & (row < first + 2 * channels) & (row % 2 == half)
            blocks.append(jnp.where(keep, base, 0.0))
    noise_lift = jnp.concatenate(blocks, axis=1).astype(BF16)
    cond_lift = jnp.concatenate(
        [jnp.where((row >= noise_rows) & (row % 2 == half), base, 0.0) for half in range(2)], axis=1
    ).astype(BF16)
    order = one_hot((col_total, col_total), lambda r, c: c == POOL * (r % offsets) + r // offsets)
    for pair in range(4):
        low = jnp.concatenate([nlow_ref[pair], clow_ref[pair]], axis=0)
        turned = mxu(order, low, NT).astype(BF16)
        cond = mxu(turned, cond_lift)
        act = in_gain * mxu(turned, noise_lift) + jnp.concatenate([cond] * members, axis=1)
        act = act.astype(BF16).astype(F32)
        for phase in range(POOL):
            for member in range(members):
                for half in range(2):
                    first = (member * 2 + half) * width
                    field_ref[phase, pair * members + member, half, pad : pad + offsets] = act[
                        phase * offsets : (phase + 1) * offsets, first : first + width
                    ]

    lanes = 128
    head_wide = one_hot((channels, lanes), lambda r, c: (c % channels == r) & (c < 4 * feat_rows))
    head_wide = mxu(head_ref[...], head_wide, TN)
    lane = iota(head_wide.shape, 1)
    heads = []
    for pair in range(2):
        for member in range(members):
            for half in range(2):
                first = (2 * pair + half) * feat_rows + member * channels
                keep = (lane >= first) & (lane < first + channels)
                heads.append(jnp.where(keep, head_wide, 0.0))
    heads = jnp.concatenate(heads, axis=0).astype(BF16)

    group = GROUP
    slots = 4 * members
    for rows in (slice(0, 8), slice(8 + block_cols, 16 + block_cols)):
        stage_ref[:, :, rows] = jnp.zeros(stage_ref.shape[:2] + (8, width), F32)
    loads[0].wait()
    build_taps(conv_ref, taps_ref)
    loads[1].wait()
    wide_ref[:, :patch] = weight_ref[...].astype(F32)
    field_ref[:, slots] = jnp.zeros(field_ref.shape[:1] + field_ref.shape[2:], F32)
    stride = group * members * block_cols
    reach = 3 * lanes

    def note(index, found):
        offset = index // slot_total
        slot = index - offset * slot_total
        live = slot < table_ref[offset, 0, slot_total]

        @pl.when(live)
        def _():
            list_ref[found] = index

        return found + live.astype(jnp.int32)

    def blank(index, carry):
        list_ref[index] = 0
        return carry

    lax.fori_loop(0, list_ref.shape[0], blank, 0)
    live_total = lax.fori_loop(0, span * slot_total, note, 0)

    def step(turn, carry):
        pieces = []
        for at in range(group):
            place = turn * group + at
            index = list_ref[place]
            offset = index // slot_total
            column = table_ref[offset, 0, index - offset * slot_total]
            pieces.append((offset, column, place < live_total))
        edge_cell = iota((8, width), 0)
        parts = []
        for tap in range(3):
            sides = []
            for half in range(2):
                rows = []
                for pair in range(4):
                    for offset, column, _ in pieces:
                        phase = column & (POOL - 1)
                        window = pl.ds((column >> 2) + pad + tap - 1, block_cols)
                        for member in range(members):
                            which = pair * members + member
                            if pair == 0:
                                which = jnp.where(offset == 0, slots, which)
                            if pair == 3:
                                which = jnp.where(offset == span - 1, slots, which)
                            at = field_ref[phase, which, half, window, :]
                            if tap == 0:
                                at = jnp.concatenate([jnp.where(edge_cell == 0, 0.0, at[:8]), at[8:]], axis=0)
                            if tap == 2:
                                at = jnp.concatenate([at[:-8], jnp.where(edge_cell == 7, 0.0, at[-8:])], axis=0)
                            rows.append(at)
                sides.append(jnp.concatenate(rows, axis=0))
            parts.append(jnp.concatenate(sides, axis=1).astype(BF16))
        act = residual_pairs(parts, taps_ref[0], stride).astype(F32)
        cells = []
        for half in range(2):
            runs = []
            for pair in range(3):
                for at, (offset, _, _) in enumerate(pieces):
                    for member in range(members):
                        first = len(runs) * block_cols
                        run = act[first : first + block_cols, half * width : (half + 1) * width]
                        if pair == 0 and half == 0:
                            run = jnp.where(offset == 0, 0.0, run)
                        if pair == 2 and half == 1:
                            run = jnp.where(offset == span - 1, 0.0, run)
                        runs.append(run)
            cells.append(runs)
        parts = shifts(cells, lambda half, at: stage_ref.at[half, at])
        act = residual_pairs(parts, taps_ref[1], stride).astype(F32)
        rows = []
        for at in range(group):
            sides = []
            for pair in range(2):
                for member in range(members):
                    first = ((pair * group + at) * members + member) * block_cols
                    sides.append(act[first : first + block_cols])
            rows.append(jnp.concatenate(sides, axis=1))
        terms = mxu(jnp.concatenate(rows, axis=0).astype(BF16), heads)
        cols = iota((block_cols, reach), 1)
        blocks = iota((block_cols, reach), 0)
        for at, (offset, column, live) in enumerate(pieces):
            term = terms[at * block_cols : (at + 1) * block_cols]
            high = term.astype(BF16)
            low = (term - high.astype(F32)).astype(BF16)
            first = jnp.minimum(column // lanes, col_total // lanes - 3) * lanes
            inner = column - first
            span_cols = pl.ds(pl.multiple_of(first, lanes), reach)
            place = jnp.where(((cols - inner) >> 2) == blocks, 1.0, 0.0).astype(BF16)
            placed = mxu(high, place, TN) + mxu(low, place, TN)
            top = pl.multiple_of(offset * strip_rows, strip_rows)
            weights = pltpu.roll(wide_ref[pl.ds(top, strip_rows), :], inner, axis=1)
            weights = jnp.where(live, weights, 0.0)
            den_ref[:, span_cols] += weights
            for row in range(strip_rows):
                below = (row // POOL) * feat_rows
                acc_ref[row, :, span_cols] += weights[row : row + 1, :] * placed[below : below + feat_rows, :]
        return carry

    lax.fori_loop(0, (live_total + group - 1) // group, step, 0)

    loads[2].wait()
    loads[3].wait()
    denom = den_ref[...]
    scale = 1.0 / jnp.maximum(denom, 1.0)
    for channel in range(channels):
        outs = []
        for member in range(members):
            at = member * channels + channel
            numer = skip_gain * noise_ref[at].astype(F32) * denom + out_gain * acc_ref[:, at, :]
            outs.append(mean_ref[channel] + numer * scale)
        ens_mean = sum(outs) * (1.0 / members)
        out_mean_ref[channel] = ens_mean
        out_var_ref[channel] = sum((out - ens_mean) ** 2 for out in outs) * (1.0 / members)


def patches(tables, nlow, clow, mean, noise, weights, lift, conv, head, slot_total):
    feat_rows, strip_rows, col_total = noise.shape
    layers, _, width, _ = conv.shape
    members = feat_rows // mean.shape[0]
    vmem = pl.BlockSpec(memory_space=pltpu.VMEM)
    far = pl.BlockSpec(memory_space=pl.ANY)
    return pl.pallas_call(
        functools.partial(patch_kernel, slot_total),
        out_shape=(jax.ShapeDtypeStruct(mean.shape, F32),) * 2,
        in_specs=[pl.BlockSpec(memory_space=pltpu.SMEM), vmem, vmem, far, far, far, vmem, far, vmem],
        out_specs=(vmem, vmem),
        scratch_shapes=[
            pltpu.VMEM((layers, 12 * width, 2 * width), BF16),
            pltpu.VMEM((POOL, 4 * members + 1, 2, col_total // POOL + 16, width), F32),
            pltpu.VMEM((weights.shape[0], 3 * 128), F32),
            pltpu.VMEM((strip_rows, feat_rows, col_total), F32),
            pltpu.VMEM((strip_rows, col_total), F32),
            pltpu.VMEM((2, GROUP * 3 * members, weights.shape[0] // POOL + 16, width), F32),
            pltpu.VMEM(mean.shape, F32),
            pltpu.VMEM(noise.shape, BF16),
            pltpu.VMEM(weights.shape, jnp.int32),
            pltpu.VMEM(conv.shape, BF16),
            pltpu.SemaphoreType.DMA((4,)),
            pltpu.SMEM((weights.shape[0] // strip_rows * slot_total + GROUP,), jnp.int32),
        ],
        name="patches",
    )(tables, nlow, clow, mean, noise, weights, lift, conv, head)


def local(
    coarse,
    noise_field,
    anchors,
    counts,
    blend_weights,
    regress_lift,
    regress_conv,
    regress_head,
    denoise_lift,
    denoise_conv,
    denoise_head,
):
    members, channels, strip_rows, col_total = noise_field.shape
    span = blend_weights.shape[0] // strip_rows
    slot_total = anchors.shape[1]
    noise = noise_field.reshape(members * channels, strip_rows, col_total)
    table = jnp.concatenate([anchors, counts[:, None]], axis=1)
    table = jnp.pad(table, ((0, 0), (0, 127 - slot_total)))[None]
    nlow, clow, mean, tables = edge(coarse, noise, table, regress_lift, regress_conv, regress_head.T, span)
    return patches(
        tables, nlow, clow, mean, noise, blend_weights, denoise_lift, denoise_conv, denoise_head.T, slot_total
    )


def solution(mesh):
    in_specs = (
        P(None, ("groups", "tile"), None),
        P(None, None, ("groups", "tile"), None),
        P(("groups", "tile"), None),
        P(("groups", "tile")),
        P(),
        P(),
        P(),
        P(),
        P(),
        P(),
        P(),
    )
    out_specs = (P(None, ("groups", "tile"), None), P(None, ("groups", "tile"), None))
    return jax.shard_map(local, mesh=mesh, in_specs=in_specs, out_specs=out_specs, check_vma=False)
```

```python
import functools
import math

import jax
import jax.numpy as jnp
from jax import lax
from jax.experimental import pallas as pl
from jax.experimental.pallas import tpu as pltpu
from jax.sharding import PartitionSpec as P

POOL = 4
PAIR = 2 * POOL
GROUP = 3

skip_gain = 0.2
out_gain = 0.5 / math.sqrt(1.25)
in_gain = 1.0 / math.sqrt(1.25)

BF16 = jnp.bfloat16
F32 = jnp.float32
NN = (((1,), (0,)), ((), ()))
NT = (((1,), (1,)), ((), ()))
TN = (((0,), (0,)), ((), ()))


def mxu(lhs, rhs, dims=NN):
    return lax.dot_general(lhs, rhs, dims, preferred_element_type=F32)


def iota(shape, axis):
    return lax.broadcasted_iota(jnp.int32, shape, axis)


def one_hot(shape, rule):
    return jnp.where(rule(iota(shape, 0), iota(shape, 1)), 1.0, 0.0).astype(BF16)


def pool_of(pairs, channels):
    depth = PAIR * pairs

    def rule(row, column):
        pair = row // (2 * channels)
        channel = row % (2 * channels) // 2
        block = 2 * pair + row % 2
        return (channel == column // depth) & (block == column % depth // POOL)

    return one_hot((2 * pairs * channels, depth * channels), rule)


def pooled(rule, cells):
    cols = cells.shape[-1]
    sums = mxu(rule, cells.reshape(-1, cols))
    sums = sums + pltpu.roll(sums, cols - 1, 1)
    sums = sums + pltpu.roll(sums, cols - 2, 1)
    return sums * (1.0 / (POOL * POOL))


def build_taps(conv_ref, taps_ref):
    width = conv_ref.shape[2]
    for layer in range(conv_ref.shape[0]):
        for tap in range(3):
            for row_in in range(4):
                for row_out in range(2):
                    at = row_in - row_out
                    rows = pl.ds((tap * 4 + row_in) * width, width)
                    block = jnp.zeros((width, width), BF16)
                    if 0 <= at < 3:
                        block = conv_ref[layer, 3 * at + tap]
                    if tap * 4 + row_in >= 6:
                        block = -block
                    taps_ref[layer, rows, row_out * width : (row_out + 1) * width] = block


def shifts(cells, holds):
    parts = [[], [], []]
    for half, runs in enumerate(cells):
        rows = [[], [], []]
        for at, run in enumerate(runs):
            count = run.shape[0]
            hold = holds(half, at)
            hold[8 : 8 + count] = run
            rows[0].append(hold[7 : 7 + count])
            rows[1].append(run)
            rows[2].append(hold[9 : 9 + count])
        for tap in range(3):
            parts[tap].append(jnp.concatenate(rows[tap], axis=0))
    return [jnp.concatenate(sides, axis=1).astype(BF16) for sides in parts]


def residual_pairs(parts, taps, stride):
    total, lanes = parts[0].shape
    count = total - stride
    half = lanes // 2
    pieces = [piece for part in parts for piece in (part[:count], part[stride:])]
    depth = taps.shape[0] // 2
    term = mxu(jnp.concatenate(pieces[:3], axis=1), taps[:depth])
    term = term - mxu(jnp.concatenate(pieces[3:], axis=1), taps[depth:])
    center = jnp.concatenate([parts[1][:count, half:], parts[1][stride:, :half]], axis=1)
    term = center.astype(F32) + term * jax.nn.sigmoid(term)
    return term.astype(BF16)


def fetch(pairs, sems):
    copies = [pltpu.make_async_copy(source, target, sems.at[at]) for at, (source, target) in enumerate(pairs)]
    for copy in copies:
        copy.start()
    return copies


def edge_kernel(
    span,
    coarse_ref,
    noise_ref,
    table_ref,
    lift_ref,
    conv_ref,
    head_ref,
    nlow_ref,
    clow_ref,
    mean_ref,
    tables_ref,
    rows_ref,
    halo_ref,
    own_ref,
    far_ref,
    taps_ref,
    stage_ref,
    send_sem,
    recv_sem,
):
    channels, strip_rows, col_total = coarse_ref.shape
    width = lift_ref.shape[1]
    block_cols = col_total // POOL
    block_rows = strip_rows // POOL
    mine = lax.axis_index("tile")
    count = lax.axis_size("tile")
    barrier = pltpu.get_barrier_semaphore()

    def holds(place):
        return jnp.logical_and(place >= 0, place < count)

    moves = [
        (rows_ref.at[1], halo_ref.at[0], 1),
        (rows_ref.at[0], halo_ref.at[1], -1),
        (own_ref.at[0], far_ref.at[0], 1),
        (own_ref.at[1], far_ref.at[1], -1),
        (nlow_ref.at[2], nlow_ref.at[0], 1),
        (nlow_ref.at[1], nlow_ref.at[3], -1),
    ]
    moves = moves + [(table_ref.at[0], tables_ref.at[at], at) for at in range(span - 1, 0, -1)]
    steps = sorted({move[2] for move in moves})
    for step in steps:
        pl.semaphore_signal(
            barrier,
            inc=1,
            device_id={"tile": lax.rem(mine - step + count, count)},
            device_id_type=pl.DeviceIdType.MESH,
        )

    def copy_of(index):
        source, target, step = moves[index]
        return pltpu.make_async_remote_copy(
            src_ref=source,
            dst_ref=target,
            send_sem=send_sem.at[index],
            recv_sem=recv_sem.at[index],
            device_id={"tile": mine + step},
            device_id_type=pl.DeviceIdType.MESH,
        )

    def start(index):
        @pl.when(holds(mine + moves[index][2]))
        def _():
            copy_of(index).start()

    def arrive(index):
        @pl.when(holds(mine - moves[index][2]))
        def _():
            copy_of(index).wait_recv()

    def leave(index):
        @pl.when(holds(mine + moves[index][2]))
        def _():
            copy_of(index).wait_send()

    def clear(index):
        target, step = moves[index][1:]

        @pl.when(jnp.logical_not(holds(mine - step)))
        def _():
            target[...] = jnp.zeros(target.shape, target.dtype)

    low = pooled(pool_of(2, 2 * channels), noise_ref[...]).astype(BF16)
    for pair in range(2):
        nlow_ref[1 + pair] = low[pair * 4 * channels : (pair + 1) * 4 * channels]
    pick = one_hot((block_cols, col_total), lambda r, c: c == POOL * r)
    spread = one_hot((block_cols, col_total), lambda r, c: c // POOL == r)
    lift_rows = mxu(one_hot((2 * channels, channels), lambda r, c: r // 2 == c), lift_ref[...])
    at_row = iota(lift_rows.shape, 0) % 2
    lift_pair = jnp.concatenate([jnp.where(at_row == half, lift_rows, 0.0) for half in range(2)], axis=1)
    lift_pair = lift_pair.astype(BF16)
    head_rows = mxu(one_hot((PAIR * channels, channels), lambda r, c: r // PAIR == c), head_ref[...])
    at_row = iota(head_rows.shape, 0) % PAIR // POOL
    head_pair = jnp.concatenate([jnp.where(at_row == half, head_rows, 0.0) for half in range(2)], axis=1)
    head_pair = head_pair.astype(BF16)
    stage_ref[:, :, :8] = jnp.zeros(stage_ref.shape[:2] + (8, width), F32)
    stage_ref[:, :, 8 + block_cols :] = jnp.zeros(stage_ref.shape[:2] + (8, width), F32)

    strip_rule = pool_of(2, channels)
    pair_rule = pool_of(1, channels)
    low_rows = 2 * channels

    def lifted(low):
        act = mxu(mxu(pick, low, NT).astype(BF16), lift_pair)
        return act.astype(BF16).astype(F32)

    own = coarse_ref[...].astype(F32)
    own = [own[:, :PAIR], own[:, PAIR:]]
    low = pooled(strip_rule, coarse_ref[...]).astype(BF16)
    own_low = [low[:low_rows], low[low_rows:]]
    for pair in range(2):
        rows_ref[pair] = own[pair].reshape(PAIR * channels, col_total).astype(BF16)
        own_ref[pair] = own_low[pair]
    build_taps(conv_ref, taps_ref)
    own_act = [lifted(low) for low in own_low]
    for index in range(len(moves)):
        clear(index)
    tables_ref[0] = table_ref[0]
    pl.semaphore_wait(barrier, len(steps))
    for index in list(range(6, len(moves))) + list(range(4)):
        start(index)
    for index in range(4):
        arrive(index)
    start(4)
    start(5)
    near = [pooled(pair_rule, halo_ref[at]).astype(BF16) for at in range(2)]
    acts = [lifted(far_ref[0]), lifted(near[0])] + own_act + [lifted(near[1]), lifted(far_ref[1])]
    domain_rows = count * block_rows
    layers = conv_ref.shape[0]
    cells = [[act[:, half * width : (half + 1) * width] for act in acts] for half in range(2)]
    for layer in range(layers):
        parts = shifts(cells, lambda half, at: stage_ref.at[half, at])
        act = residual_pairs(parts, taps_ref[layer], block_cols).astype(F32)
        cells = []
        for half in range(2):
            runs = []
            for pair in range(act.shape[0] // block_cols):
                run = act[pair * block_cols : (pair + 1) * block_cols, half * width : (half + 1) * width]
                row = 2 * pair + half + layer + 1 - block_rows
                if not 0 <= row < block_rows:
                    place = mine * block_rows + row
                    run = jnp.where(jnp.logical_and(place >= 0, place < domain_rows), run, 0.0)
                runs.append(run)
            cells.append(runs)

    above, below = [halo_ref[at].astype(F32).reshape(own[0].shape) for at in range(2)]
    fields = [above] + own + [below]
    lows = near[:1] + own_low + near[1:]
    for pair in range(4):
        act = jnp.concatenate([cells[half][pair] for half in range(2)], axis=1).astype(BF16)
        rest = mxu(head_pair, act, NT)
        wide = 0.0
        for _ in range(3):
            part = rest.astype(BF16)
            wide = wide + mxu(part, spread)
            rest = rest - part.astype(F32)
        mean = fields[pair] + wide.reshape(channels, PAIR, col_total)
        if 1 <= pair <= 2:
            mean_ref[:, (pair - 1) * PAIR : pair * PAIR] = mean
        low = pooled(pair_rule, mean.reshape(PAIR * channels, col_total).astype(BF16))
        clow_ref[pair] = jnp.concatenate([low, lows[pair].astype(F32)], axis=0).astype(BF16)
    for index in range(4, len(moves)):
        arrive(index)
    for index in range(len(moves)):
        leave(index)


def edge(coarse, noise, table, lift, conv, head, span):
    channels, strip_rows, col_total = coarse.shape
    layers, _, width, _ = conv.shape
    vmem = pl.BlockSpec(memory_space=pltpu.VMEM)
    copies = span + 5
    return pl.pallas_call(
        functools.partial(edge_kernel, span),
        out_shape=(
            jax.ShapeDtypeStruct((4, 4 * channels, col_total), BF16),
            jax.ShapeDtypeStruct((4, 4 * channels, col_total), BF16),
            jax.ShapeDtypeStruct(coarse.shape, F32),
            jax.ShapeDtypeStruct((span, 1, 128), jnp.int32),
        ),
        in_specs=[vmem] * 6,
        out_specs=(vmem,) * 4,
        scratch_shapes=[
            pltpu.VMEM((2, PAIR * channels, col_total), BF16),
            pltpu.VMEM((2, PAIR * channels, col_total), BF16),
            pltpu.VMEM((2, 2 * channels, col_total), BF16),
            pltpu.VMEM((2, 2 * channels, col_total), BF16),
            pltpu.VMEM((layers, 12 * width, 2 * width), BF16),
            pltpu.VMEM((2, 3 * strip_rows // PAIR, col_total // POOL + 16, width), F32),
            pltpu.SemaphoreType.DMA((copies,)),
            pltpu.SemaphoreType.DMA((copies,)),
        ],
        compiler_params=pltpu.CompilerParams(collective_id=0, has_side_effects=True),
        name="edge",
    )(coarse, noise, table, lift, conv, head)


def patch_kernel(
    slot_total,
    table_ref,
    nlow_ref,
    clow_ref,
    mean_hbm,
    noise_hbm,
    weight_hbm,
    lift_ref,
    conv_hbm,
    head_ref,
    out_mean_ref,
    out_var_ref,
    taps_ref,
    field_ref,
    wide_ref,
    acc_ref,
    den_ref,
    stage_ref,
    mean_ref,
    noise_ref,
    weight_ref,
    conv_ref,
    load_sem,
    list_ref,
):
    feat_rows, strip_rows, col_total = noise_ref.shape
    channels = mean_ref.shape[0]
    members = feat_rows // channels
    width = lift_ref.shape[1]
    patch = weight_ref.shape[0]
    span = patch // strip_rows
    block_cols = patch // POOL
    offsets = col_total // POOL
    pad = 8

    loads = fetch(
        [(conv_hbm, conv_ref), (weight_hbm, weight_ref), (mean_hbm, mean_ref), (noise_hbm, noise_ref)], load_sem
    )
    acc_ref[...] = jnp.zeros_like(acc_ref)
    den_ref[...] = jnp.zeros_like(den_ref)
    wide_ref[...] = jnp.zeros_like(wide_ref)

    low_rows = 2 * feat_rows + 4 * channels
    noise_rows = 2 * feat_rows

    def source(row, column):
        noise_at = (row // 2) % channels
        cond_at = channels + (row - noise_rows) // 2
        return column == jnp.where(row < noise_rows, noise_at, cond_at)

    base = mxu(one_hot((low_rows, 3 * channels), source), lift_ref[...])
    row = iota(base.shape, 0)
    blocks = []
    for member in range(members):
        first = 2 * channels * member
        for half in range(2):
            keep = (row >= first) & (row < first + 2 * channels) & (row % 2 == half)
            blocks.append(jnp.where(keep, base, 0.0))
    noise_lift = jnp.concatenate(blocks, axis=1).astype(BF16)
    cond_lift = jnp.concatenate(
        [jnp.where((row >= noise_rows) & (row % 2 == half), base, 0.0) for half in range(2)], axis=1
    ).astype(BF16)
    order = one_hot((col_total, col_total), lambda r, c: c == POOL * (r % offsets) + r // offsets)
    for pair in range(4):
        low = jnp.concatenate([nlow_ref[pair], clow_ref[pair]], axis=0)
        turned = mxu(order, low, NT).astype(BF16)
        cond = mxu(turned, cond_lift)
        act = in_gain * mxu(turned, noise_lift) + jnp.concatenate([cond] * members, axis=1)
        act = act.astype(BF16).astype(F32)
        for phase in range(POOL):
            for member in range(members):
                for half in range(2):
                    first = (member * 2 + half) * width
                    field_ref[phase, pair * members + member, half, pad : pad + offsets] = act[
                        phase * offsets : (phase + 1) * offsets, first : first + width
                    ]

    lanes = 128
    head_wide = one_hot((channels, lanes), lambda r, c: (c % channels == r) & (c < 4 * feat_rows))
    head_wide = mxu(head_ref[...], head_wide, TN)
    lane = iota(head_wide.shape, 1)
    heads = []
    for pair in range(2):
        for member in range(members):
            for half in range(2):
                first = (2 * pair + half) * feat_rows + member * channels
                keep = (lane >= first) & (lane < first + channels)
                heads.append(jnp.where(keep, head_wide, 0.0))
    heads = jnp.concatenate(heads, axis=0).astype(BF16)

    group = GROUP
    slots = 4 * members
    for rows in (slice(0, 8), slice(8 + block_cols, 16 + block_cols)):
        stage_ref[:, :, rows] = jnp.zeros(stage_ref.shape[:2] + (8, width), F32)
    loads[0].wait()
    build_taps(conv_ref, taps_ref)
    loads[1].wait()
    wide_ref[:, :patch] = weight_ref[...].astype(F32)
    field_ref[:, slots] = jnp.zeros(field_ref.shape[:1] + field_ref.shape[2:], F32)
    stride = group * members * block_cols
    reach = 3 * lanes

    def note(index, found):
        offset = index // slot_total
        slot = index - offset * slot_total
        live = slot < table_ref[offset, 0, slot_total]

        @pl.when(live)
        def _():
            list_ref[found] = index

        return found + live.astype(jnp.int32)

    def blank(index, carry):
        list_ref[index] = 0
        return carry

    lax.fori_loop(0, list_ref.shape[0], blank, 0)
    live_total = lax.fori_loop(0, span * slot_total, note, 0)

    def step(turn, carry):
        pieces = []
        for at in range(group):
            place = turn * group + at
            index = list_ref[place]
            offset = index // slot_total
            column = table_ref[offset, 0, index - offset * slot_total]
            pieces.append((offset, column, place < live_total))
        edge_cell = iota((8, width), 0)
        parts = []
        for tap in range(3):
            sides = []
            for half in range(2):
                rows = []
                for pair in range(4):
                    for offset, column, _ in pieces:
                        phase = column & (POOL - 1)
                        window = pl.ds((column >> 2) + pad + tap - 1, block_cols)
                        for member in range(members):
                            which = pair * members + member
                            if pair == 0:
                                which = jnp.where(offset == 0, slots, which)
                            if pair == 3:
                                which = jnp.where(offset == span - 1, slots, which)
                            at = field_ref[phase, which, half, window, :]
                            if tap == 0:
                                at = jnp.concatenate([jnp.where(edge_cell == 0, 0.0, at[:8]), at[8:]], axis=0)
                            if tap == 2:
                                at = jnp.concatenate([at[:-8], jnp.where(edge_cell == 7, 0.0, at[-8:])], axis=0)
                            rows.append(at)
                sides.append(jnp.concatenate(rows, axis=0))
            parts.append(jnp.concatenate(sides, axis=1).astype(BF16))
        act = residual_pairs(parts, taps_ref[0], stride).astype(F32)
        cells = []
        for half in range(2):
            runs = []
            for pair in range(3):
                for at, (offset, _, _) in enumerate(pieces):
                    for member in range(members):
                        first = len(runs) * block_cols
                        run = act[first : first + block_cols, half * width : (half + 1) * width]
                        if pair == 0 and half == 0:
                            run = jnp.where(offset == 0, 0.0, run)
                        if pair == 2 and half == 1:
                            run = jnp.where(offset == span - 1, 0.0, run)
                        runs.append(run)
            cells.append(runs)
        parts = shifts(cells, lambda half, at: stage_ref.at[half, at])
        act = residual_pairs(parts, taps_ref[1], stride).astype(F32)
        rows = []
        for at in range(group):
            sides = []
            for pair in range(2):
                for member in range(members):
                    first = ((pair * group + at) * members + member) * block_cols
                    sides.append(act[first : first + block_cols])
            rows.append(jnp.concatenate(sides, axis=1))
        terms = mxu(jnp.concatenate(rows, axis=0).astype(BF16), heads)
        cols = iota((block_cols, reach), 1)
        blocks = iota((block_cols, reach), 0)
        for at, (offset, column, live) in enumerate(pieces):
            term = terms[at * block_cols : (at + 1) * block_cols]
            high = term.astype(BF16)
            low = (term - high.astype(F32)).astype(BF16)
            first = jnp.minimum(column // lanes, col_total // lanes - 3) * lanes
            inner = column - first
            span_cols = pl.ds(pl.multiple_of(first, lanes), reach)
            place = jnp.where(((cols - inner) >> 2) == blocks, 1.0, 0.0).astype(BF16)
            placed = mxu(high, place, TN) + mxu(low, place, TN)
            top = pl.multiple_of(offset * strip_rows, strip_rows)
            weights = pltpu.roll(wide_ref[pl.ds(top, strip_rows), :], inner, axis=1)
            weights = jnp.where(live, weights, 0.0)
            den_ref[:, span_cols] += weights
            for row in range(strip_rows):
                below = (row // POOL) * feat_rows
                acc_ref[row, :, span_cols] += weights[row : row + 1, :] * placed[below : below + feat_rows, :]
        return carry

    lax.fori_loop(0, (live_total + group - 1) // group, step, 0)

    loads[2].wait()
    loads[3].wait()
    denom = den_ref[...]
    scale = 1.0 / jnp.maximum(denom, 1.0)
    for channel in range(channels):
        outs = []
        for member in range(members):
            at = member * channels + channel
            numer = skip_gain * noise_ref[at].astype(F32) * denom + out_gain * acc_ref[:, at, :]
            outs.append(mean_ref[channel] + numer * scale)
        ens_mean = sum(outs) * (1.0 / members)
        out_mean_ref[channel] = ens_mean
        out_var_ref[channel] = sum((out - ens_mean) ** 2 for out in outs) * (1.0 / members)


def patches(tables, nlow, clow, mean, noise, weights, lift, conv, head, slot_total):
    feat_rows, strip_rows, col_total = noise.shape
    layers, _, width, _ = conv.shape
    members = feat_rows // mean.shape[0]
    vmem = pl.BlockSpec(memory_space=pltpu.VMEM)
    far = pl.BlockSpec(memory_space=pl.ANY)
    return pl.pallas_call(
        functools.partial(patch_kernel, slot_total),
        out_shape=(jax.ShapeDtypeStruct(mean.shape, F32),) * 2,
        in_specs=[pl.BlockSpec(memory_space=pltpu.SMEM), vmem, vmem, far, far, far, vmem, far, vmem],
        out_specs=(vmem, vmem),
        scratch_shapes=[
            pltpu.VMEM((layers, 12 * width, 2 * width), BF16),
            pltpu.VMEM((POOL, 4 * members + 1, 2, col_total // POOL + 16, width), F32),
            pltpu.VMEM((weights.shape[0], 3 * 128), F32),
            pltpu.VMEM((strip_rows, feat_rows, col_total), F32),
            pltpu.VMEM((strip_rows, col_total), F32),
            pltpu.VMEM((2, GROUP * 3 * members, weights.shape[0] // POOL + 16, width), F32),
            pltpu.VMEM(mean.shape, F32),
            pltpu.VMEM(noise.shape, BF16),
            pltpu.VMEM(weights.shape, jnp.int32),
            pltpu.VMEM(conv.shape, BF16),
            pltpu.SemaphoreType.DMA((4,)),
            pltpu.SMEM((weights.shape[0] // strip_rows * slot_total + GROUP,), jnp.int32),
        ],
        name="patches",
    )(tables, nlow, clow, mean, noise, weights, lift, conv, head)


def local(
    coarse,
    noise_field,
    anchors,
    counts,
    blend_weights,
    regress_lift,
    regress_conv,
    regress_head,
    denoise_lift,
    denoise_conv,
    denoise_head,
):
    members, channels, strip_rows, col_total = noise_field.shape
    span = blend_weights.shape[0] // strip_rows
    slot_total = anchors.shape[1]
    noise = noise_field.reshape(members * channels, strip_rows, col_total)
    table = jnp.concatenate([anchors, counts[:, None]], axis=1)
    table = jnp.pad(table, ((0, 0), (0, 127 - slot_total)))[None]
    nlow, clow, mean, tables = edge(coarse, noise, table, regress_lift, regress_conv, regress_head.T, span)
    return patches(
        tables, nlow, clow, mean, noise, blend_weights, denoise_lift, denoise_conv, denoise_head.T, slot_total
    )


def solution(mesh):
    in_specs = (
        P(None, ("groups", "tile"), None),
        P(None, None, ("groups", "tile"), None),
        P(("groups", "tile"), None),
        P(("groups", "tile")),
        P(),
        P(),
        P(),
        P(),
        P(),
        P(),
        P(),
    )
    out_specs = (P(None, ("groups", "tile"), None), P(None, ("groups", "tile"), None))
    return jax.shard_map(local, mesh=mesh, in_specs=in_specs, out_specs=out_specs, check_vma=False)
```
